128 devices in a mesh: queue: 32 (over y, x, z_lo), head: 4 (over z_hi, core).
Axes of the slice: x: 4, y: 4, z: 4 (z_hi: 2, z_lo: 2; z = z_hi * 2 + z_lo), core: 2. Of those that a mesh axis runs over, the one named last changes fastest.
Arguments:
- latents: bfloat16 [64, 384, 5120], P('queue'), may hold values from -6 to 6
- control: bfloat16 [64, 384, 5120], P('queue'), may hold values from -3 to 3
- levels: int32 [64], P('queue'), may hold values from 0 to 63
- window_mask: int32 [64, 2], P('queue'), may hold values 0 or 1
- modulation: float32 [64, 3, 5120], replicated, may hold values from -3 to 3
- w_query: bfloat16 [5120, 2560], P('queue', 'head'), may hold values from -1 to 1
- w_key: bfloat16 [5120, 2560], P('queue', 'head'), may hold values from -1 to 1
- w_value: bfloat16 [5120, 2560], P('queue', 'head'), may hold values from -0.078125 to 0.078125
- w_out: bfloat16 [2560, 5120], P('head', 'queue'), may hold values from -0.125 to 0.125
- q_gain: float32 [2560], P('head'), may hold values from 0.6 to 8
- k_gain: float32 [2560], P('head'), may hold values from 0.6 to 8
Outputs:
- next_queue: float32 [64, 384, 5120], P('queue', None, 'head')
The draws below stay inside these ranges and needn't reach their ends.
All inputs are finite; a program needn't handle non-finite values. No bound on the sum of `window_mask` on one device may be relied on, other than what follows from the above.
Results may differ from the reference program's by a relative error of at most 0.019.
The reference program's roundings to bfloat16 on the way (of `normed`, `query`, `qhat`, `probs` and `attended`) count: a program that leaves them out, or rounds other values in their place, can miss the bound.
Values may be sent and summed in bfloat16 or wider, within the bound.
A program may use at most 192 MiB of HBM per device.

```python
import jax
import jax.numpy as jnp
from jax import lax

D = 5120
HEADS = 20
HD = 128
ROWS = 384
LEVELS = 64
SPANS = 64
N_HEAD = 4


def column_scales(key, spread):
    columns = HEADS * HD
    position = jnp.arange(columns, dtype=jnp.float32) / (columns - 1)
    jitter = jnp.exp(jax.random.uniform(key, (columns,), jnp.float32, -0.35, 0.35))
    return jnp.exp(jnp.log(spread) * (position - 0.5)) * jitter


def projection_draw(key):
    base = jax.random.normal(jax.random.fold_in(key, 11), (D, HEADS * HD), jnp.float32) * D ** (-0.5)
    base = jnp.clip(base, -5.0 * D ** (-0.5), 5.0 * D ** (-0.5))
    spread = 3.0
    scaled = base * column_scales(jax.random.fold_in(key, 12), spread)[None, :]
    return jnp.clip(scaled, -1.0, 1.0).astype(jnp.bfloat16)


def gain_draw(key):
    return jax.random.uniform(jax.random.fold_in(key, 22), (HEADS * HD,), jnp.float32, 0.6, 1.6)


def draw_w_query(key, part):
    return projection_draw(jax.random.fold_in(key, 1))


def draw_w_key(key, part):
    return projection_draw(jax.random.fold_in(key, 2))


def draw_q_gain(key, part):
    return gain_draw(jax.random.fold_in(key, 3))


def draw_k_gain(key, part):
    return gain_draw(jax.random.fold_in(key, 4))


def with_ends(drawn, own_key, least, high):
    longest = drawn.shape.index(max(drawn.shape))
    spots = []
    for shift in (0, 1):
        where = [jax.random.randint(jax.random.fold_in(own_key, axis), (), 0, length) for axis, length in enumerate(drawn.shape)]
        where[longest] = (where[longest] + shift) % drawn.shape[longest]
        spots.append(tuple(where))
    return drawn.at[spots[0]].set(least).at[spots[1]].set(high)


def level_of(rng, dims, shards, low, top_value):
    level = 1.0
    for dim, parts in shards:
        heights = jax.random.uniform(jax.random.fold_in(jax.random.fold_in(rng, 6), dim), (parts,), jnp.float32, low / len(shards), top_value / len(shards))
        level = level * jnp.repeat(jnp.exp(heights), dims[dim] // parts).reshape((-1,) + (1,) * (len(dims) - 1 - dim))
    return level


def noise(key, shape, scale, limit, pieces=(), kind=jnp.bfloat16):
    values = scale * jax.random.normal(key, shape, jnp.float32)
    if pieces:
        values = values * level_of(key, shape, pieces, -0.22, 0.18)
    return jnp.clip(values, -limit, limit).astype(kind)


def setup_inputs(seed: int = 0) -> dict:
    seeds = jax.random.split(jax.random.key(seed), 12)
    return {
        "latents": noise(seeds[0], (SPANS, ROWS, D), 1.0, 6.0, ((0, 32),)),
        "control": noise(seeds[1], (SPANS, ROWS, D), 0.5, 3.0, ((0, 32),)),
        "levels": with_ends(jax.random.randint(seeds[2], (SPANS,), 0, LEVELS), jax.random.fold_in(seeds[2], 1), 0, LEVELS - 1).astype(jnp.int32),
        "window_mask": with_ends((jax.random.randint(seeds[3], (SPANS, 2), 0, 4) < 3).astype(jnp.int32), jax.random.fold_in(seeds[3], 1), 0, 1),
        "modulation": noise(seeds[4], (LEVELS, 3, D), 1.0, 3.0, (), jnp.float32),
        "w_query": draw_w_query(jax.random.fold_in(seeds[11], 71), 0),
        "w_key": draw_w_key(jax.random.fold_in(seeds[11], 71), 0),
        "w_value": noise(seeds[7], (D, HEADS * HD), D ** -0.5, 0.078125, ((0, 32), (1, 4))),
        "w_out": noise(seeds[8], (HEADS * HD, D), (HEADS * HD) ** -0.5, 0.125, ((0, 4), (1, 32))),
        "q_gain": draw_q_gain(jax.random.fold_in(seeds[11], 71), 0),
        "k_gain": draw_k_gain(jax.random.fold_in(seeds[11], 71), 0),
    }


def layer_norm(hidden):
    center = hidden - lax.optimization_barrier(jnp.mean(hidden, axis=-1, keepdims=True))
    variance = lax.optimization_barrier(jnp.mean(center * center, axis=-1, keepdims=True))
    return center * lax.rsqrt(variance + 1e-06)

def gain_norm(values, gain):
    floats = values.astype(jnp.float32)
    square_mean = lax.optimization_barrier(jnp.mean(floats * floats, axis=-1, keepdims=True))
    return (floats * lax.rsqrt(square_mean + 1e-06) * gain).astype(jnp.bfloat16)

def reference(latents, control, levels, window_mask, modulation, w_query, w_key, w_value, w_out, q_gain, k_gain):
    hidden = latents.astype(jnp.float32) + control.astype(jnp.float32)
    onehot = (levels[:, None] == jnp.arange(LEVELS, dtype=jnp.int32)[None, :]).astype(jnp.float32)
    level_mods = jnp.dot(onehot, modulation.reshape(LEVELS, 3 * D), precision=lax.Precision.HIGHEST).reshape(SPANS, 3, D)
    offset_mod = level_mods[:, 0][:, None, :]
    scale_mod = level_mods[:, 1][:, None, :]
    gate_mod = level_mods[:, 2][:, None, :]
    normed = (layer_norm(hidden) * (1.0 + scale_mod) + offset_mod).astype(jnp.bfloat16)
    flat_rows = normed.reshape(SPANS * ROWS, D)
    query = jnp.dot(flat_rows, w_query, preferred_element_type=jnp.float32).astype(jnp.bfloat16)
    keyproj = jnp.dot(flat_rows, w_key, preferred_element_type=jnp.float32).astype(jnp.bfloat16)
    valueproj = jnp.dot(flat_rows, w_value, preferred_element_type=jnp.float32).astype(jnp.bfloat16)
    qhat = gain_norm(query, q_gain).reshape(SPANS, ROWS, HEADS, HD)
    khat = gain_norm(keyproj, k_gain).reshape(SPANS, ROWS, HEADS, HD)
    values = valueproj.reshape(SPANS, ROWS, HEADS, HD)
    padding = jnp.zeros((2, ROWS, HEADS, HD), jnp.bfloat16)
    keys_padded = jnp.concatenate([padding, khat], axis=0)
    values_padded = jnp.concatenate([padding, values], axis=0)
    span_ids = jnp.arange(SPANS, dtype=jnp.int32)
    seen_far = (window_mask[:, 0] == 1) & (span_ids >= 2)
    seen_near = (window_mask[:, 1] == 1) & (span_ids >= 1)
    seen = jnp.stack([seen_far, seen_near, jnp.ones((SPANS,), dtype=bool)], axis=1)

    def one_span(packed):
        query_span, seen_row, span_id = packed
        key_window = lax.dynamic_slice(keys_padded, (span_id, jnp.int32(0), jnp.int32(0), jnp.int32(0)), (3, ROWS, HEADS, HD)).reshape(3 * ROWS, HEADS, HD)
        value_window = lax.dynamic_slice(values_padded, (span_id, jnp.int32(0), jnp.int32(0), jnp.int32(0)), (3, ROWS, HEADS, HD)).reshape(3 * ROWS, HEADS, HD)
        scores = jnp.einsum('qhd,khd->hqk', query_span.astype(jnp.float32), key_window.astype(jnp.float32)) * HD ** (-0.5)
        key_seen = jnp.repeat(seen_row, ROWS)
        scores = jnp.where(key_seen[None, None, :], scores, -1e+30)
        top = lax.optimization_barrier(jnp.max(scores, axis=-1, keepdims=True))
        expo = jnp.exp(scores - top)
        probs = (expo / lax.optimization_barrier(jnp.sum(expo, axis=-1, keepdims=True))).astype(jnp.bfloat16)
        attended = jnp.einsum('hqk,khd->qhd', probs.astype(jnp.float32), value_window.astype(jnp.float32))
        return attended.astype(jnp.bfloat16).reshape(ROWS, HEADS * HD)
    attended = lax.map(one_span, (qhat, seen, span_ids)).reshape(SPANS * ROWS, HEADS * HD)
    group_width = HEADS * HD // N_HEAD
    branch = jnp.zeros((SPANS * ROWS, D), jnp.float32)
    for group in range(N_HEAD):
        partial_out = jnp.dot(attended[:, group * group_width:(group + 1) * group_width], w_out[group * group_width:(group + 1) * group_width], preferred_element_type=jnp.float32)
        rounded = lax.optimization_barrier(partial_out.astype(jnp.bfloat16))
        branch = branch + rounded.astype(jnp.float32)
    updated = hidden + gate_mod * branch.reshape(SPANS, ROWS, D)
    return jnp.roll(updated, 1, axis=0)
```

```python
import functools

import jax
import jax.numpy as jnp
from jax import lax
from jax.experimental import pallas as pl
from jax.experimental.pallas import tpu as pltpu
from jax.sharding import PartitionSpec as P

HD = 128
MESH = pl.DeviceIdType.MESH


def queue_at(x, y, zl):
    return ((y % 4) * 4 + x % 4) * 2 + zl


def gather_kernel(wq, wk, wv, wo, oq, ok, ov, oo, lsem, zs, zr, asnd, arcv, bsnd, brcv):
    q = lax.axis_index("queue")
    h = lax.axis_index("head")
    zl = q % 2
    x = (q // 2) % 4
    y = q // 8
    srcs = (wq, wk, wv, wo)
    dsts = (oq, ok, ov, oo)

    def near(axis, by):
        return (x + by, y) if axis == 0 else (x, y + by)

    barrier = pltpu.get_barrier_semaphore()
    peers = [(queue_at(x, y, 1 - zl), h)]
    for axis in (0, 1):
        for by in (1, 2, 3):
            px, py = near(axis, by)
            peers.append((queue_at(px, py, zl), h))
    for peer in peers:
        pl.semaphore_signal(barrier, inc=1, device_id=peer, device_id_type=MESH)
    pl.semaphore_wait(barrier, len(peers))

    def rows(ref, first, count):
        return ref.at[pl.ds(first * 160, count * 160), :]

    sends = []
    locals_ = []
    for m in range(4):
        c = pltpu.make_async_copy(srcs[m], rows(dsts[m], q, 1), lsem.at[m])
        c.start()
        locals_.append(c)

    def remote(src, dst, ss, rs, dev):
        return pltpu.make_async_remote_copy(
            src_ref=src, dst_ref=dst, send_sem=ss, recv_sem=rs, device_id=dev, device_id_type=MESH
        )

    zcopies = []
    for m in range(4):
        c = remote(srcs[m], rows(dsts[m], q, 1), zs.at[m], zr.at[m], (queue_at(x, y, 1 - zl), h))
        c.start()
        zcopies.append(c)
        sends.append(c)
    first_axis = (0, 0, 1, 1)

    def step_a(m, which, sender):
        axis = first_axis[m]
        for by in (1, 3, 2):
            px, py = near(axis, by)
            qs = queue_at(x, y, zl if which == 0 else 1 - zl)
            src = srcs[m] if which == 0 else rows(dsts[m], qs, 1)
            c = remote(
                src,
                rows(dsts[m], qs, 1),
                asnd.at[m, which, by - 1],
                arcv.at[m, which, by - 1],
                (queue_at(px, py, zl), h),
            )
            c.start()
            sends.append(c)

    def step_b(m, frm):
        axis = first_axis[m]
        sx, sy = near(axis, -frm)
        block = rows(dsts[m], queue_at(sx, sy, 0), 2)
        for by in (1, 3, 2):
            px, py = near(1 - axis, by)
            c = remote(
                block,
                block,
                bsnd.at[m, frm, by - 1],
                brcv.at[m, frm, by - 1],
                (queue_at(px, py, zl), h),
            )
            c.start()
            sends.append(c)

    for m in range(4):
        step_a(m, 0, sends)
    for m in range(4):
        zcopies[m].wait_recv()
        step_a(m, 1, sends)
    for m in range(4):
        locals_[m].wait()
        step_b(m, 0)
    for by in (1, 3, 2):
        for m in range(4):
            sx, sy = near(first_axis[m], -by)
            for which in (0, 1):
                qs = queue_at(sx, sy, zl if which == 0 else 1 - zl)
                block = rows(dsts[m], qs, 1)
                remote(
                    block, block, asnd.at[m, which, by - 1], arcv.at[m, which, by - 1], (q, h)
                ).wait_recv()
            step_b(m, by)
    for frm in range(4):
        for by in (1, 3, 2):
            for m in range(4):
                axis = first_axis[m]
                sx, sy = near(axis, -frm)
                if axis == 0:
                    sy = sy - by
                else:
                    sx = sx - by
                block = rows(dsts[m], queue_at(sx, sy, 0), 2)
                remote(
                    block, block, bsnd.at[m, frm, by - 1], brcv.at[m, frm, by - 1], (q, h)
                ).wait_recv()
    for c in sends:
        c.wait_send()


def gather_weights(wq, wk, wv, wo_t):
    out = jax.ShapeDtypeStruct((5120, 640), jnp.bfloat16)
    return pl.pallas_call(
        gather_kernel,
        out_shape=[out] * 4,
        in_specs=[pl.BlockSpec(memory_space=pl.ANY)] * 4,
        out_specs=[pl.BlockSpec(memory_space=pl.ANY)] * 4,
        scratch_shapes=[
            pltpu.SemaphoreType.DMA((4,)),
            pltpu.SemaphoreType.DMA((4,)),
            pltpu.SemaphoreType.DMA((4,)),
            pltpu.SemaphoreType.DMA((4, 2, 3)),
            pltpu.SemaphoreType.DMA((4, 2, 3)),
            pltpu.SemaphoreType.DMA((4, 4, 3)),
            pltpu.SemaphoreType.DMA((4, 4, 3)),
        ],
        compiler_params=pltpu.CompilerParams(collective_id=0, has_side_effects=True),
        name="gather_weights",
    )(wq, wk, wv, wo_t)


def from_behind(value, axis, by):
    peers = lax.axis_size(axis)
    pairs = [(i, i + by) for i in range(peers) if 0 <= i + by < peers]
    return lax.ppermute(value, axis, pairs)


def shifted(value, axis, steps):
    count = lax.axis_size(axis)
    pairs = [(source, (source + steps) % count) for source in range(count)]
    return lax.ppermute(value, axis, pairs)


def layer_norm(hidden):
    center = hidden - jnp.mean(hidden, axis=-1, keepdims=True)
    variance = jnp.mean(center * center, axis=-1, keepdims=True)
    return center * lax.rsqrt(variance + 1e-06)


def apply_gain(values, square_sum, total_width, gain):
    floats = values.astype(jnp.float32)
    return (floats * lax.rsqrt(square_sum[:, None] / total_width + 1e-06) * gain).astype(
        jnp.bfloat16
    )


def row_squares(values):
    floats = values.astype(jnp.float32)
    return jnp.sum(floats * floats, axis=-1)


def shards(
    latents,
    control,
    levels,
    window_mask,
    modulation,
    w_query,
    w_key,
    w_value,
    w_out,
    q_gain,
    k_gain,
):
    nchunk, row_count, model_width = latents.shape
    level_count = modulation.shape[0]
    local_cols = w_query.shape[1]
    heads_local = local_cols // HD
    head_count = lax.axis_size("head")
    total_width = local_cols * head_count
    owner_index = lax.axis_index("queue")
    head_index = lax.axis_index("head")
    first_span = owner_index * nchunk
    hidden = latents.astype(jnp.float32) + control.astype(jnp.float32)
    onehot = (levels[:, None] == jnp.arange(level_count, dtype=jnp.int32)[None, :]).astype(
        jnp.float32
    )
    level_mods = jnp.dot(
        onehot, modulation.reshape(level_count, 3 * model_width), precision=lax.Precision.HIGHEST
    ).reshape(nchunk, 3, model_width)
    normed = (
        layer_norm(hidden) * (1.0 + level_mods[:, 1][:, None, :]) + level_mods[:, 0][:, None, :]
    ).astype(jnp.bfloat16)
    flat_rows = normed.reshape(nchunk * row_count, model_width)
    row_total = nchunk * row_count
    full_query, full_key, full_value, full_out = gather_weights(w_query, w_key, w_value, w_out.T)
    pieces = (full_query, full_key, full_value)
    query, keyproj, valueproj = tuple(
        (
            jnp.dot(flat_rows, piece_rows, preferred_element_type=jnp.float32)
            for piece_rows in pieces
        )
    )
    query = query.astype(jnp.bfloat16)
    keyproj = keyproj.astype(jnp.bfloat16)
    valueproj = valueproj.astype(jnp.bfloat16)
    query_sq, key_sq = lax.psum((row_squares(query), row_squares(keyproj)), "head")
    qhat = apply_gain(query, query_sq, total_width, q_gain)
    own_keys = apply_gain(keyproj, key_sq, total_width, k_gain)
    prior_keys, prior_values = from_behind((own_keys, valueproj), "queue", 1)
    key_stack = jnp.concatenate([prior_keys, own_keys], axis=0).reshape(
        2 * nchunk, row_count, heads_local, HD
    )
    value_stack = jnp.concatenate([prior_values, valueproj], axis=0).reshape(
        2 * nchunk, row_count, heads_local, HD
    )
    key_windows = jnp.stack(
        [
            key_stack[nchunk + index_span - 2 : nchunk + index_span + 1]
            for index_span in range(nchunk)
        ]
    ).reshape(nchunk, 3 * row_count, heads_local, HD)
    value_windows = jnp.stack(
        [
            value_stack[nchunk + index_span - 2 : nchunk + index_span + 1]
            for index_span in range(nchunk)
        ]
    ).reshape(nchunk, 3 * row_count, heads_local, HD)
    span_ids = first_span + jnp.arange(nchunk, dtype=jnp.int32)
    seen_far = (window_mask[:, 0] == 1) & (span_ids >= 2)
    seen_near = (window_mask[:, 1] == 1) & (span_ids >= 1)
    seen = jnp.stack([seen_far, seen_near, jnp.ones((nchunk,), dtype=bool)], axis=1)
    key_seen = jnp.repeat(seen, row_count, axis=1)
    query_spans = qhat.reshape(nchunk, row_count, heads_local, HD)
    scores = jnp.einsum(
        "cqhd,ckhd->chqk", query_spans, key_windows, preferred_element_type=jnp.float32
    ) * HD ** (-0.5)
    scores = jnp.where(key_seen[:, None, None, :], scores, -1e30)
    top = jnp.max(scores, axis=-1, keepdims=True)
    expo = jnp.exp(scores - top)
    prob_bf = (expo / jnp.sum(expo, axis=-1, keepdims=True)).astype(jnp.bfloat16)
    attended = jnp.einsum(
        "chqk,ckhd->cqhd", prob_bf, value_windows, preferred_element_type=jnp.float32
    )
    attended = attended.astype(jnp.bfloat16).reshape(row_total, local_cols)
    partial_out = lax.dot_general(
        attended,
        full_out,
        (((1,), (1,)), ((), ())),
        preferred_element_type=jnp.float32,
    )
    col_width = model_width // head_count
    hidden_cols = lax.dynamic_slice_in_dim(hidden, head_index * col_width, col_width, 2)
    gate_cols = lax.dynamic_slice_in_dim(level_mods[:, 2], head_index * col_width, col_width, 1)
    branch = (
        lax.psum_scatter(partial_out.astype(jnp.bfloat16), "head", scatter_dimension=1, tiled=True)
        .astype(jnp.float32)
        .reshape(nchunk, row_count, col_width)
    )
    updated = hidden_cols + gate_cols[:, None, :] * branch
    arrived = shifted(updated[nchunk - 1].astype(jnp.bfloat16), "queue", 1).astype(jnp.float32)
    return jnp.concatenate([arrived[None], updated[: nchunk - 1]], axis=0)


def solution(mesh):
    placed = (
        P("queue", None, None),
        P("queue", None, None),
        P("queue"),
        P("queue", None),
        P(),
        P("queue", "head"),
        P("queue", "head"),
        P("queue", "head"),
        P("head", "queue"),
        P("head"),
        P("head"),
    )
    return jax.shard_map(
        shards, mesh=mesh, in_specs=placed, out_specs=P("queue", None, "head"), check_vma=False
    )
```

```python
import functools

import jax
import jax.numpy as jnp
from jax import lax
from jax.experimental import pallas as pl
from jax.experimental.pallas import tpu as pltpu
from jax.sharding import PartitionSpec as P

HD = 128
MESH = pl.DeviceIdType.MESH
BF = jnp.bfloat16
F32 = jnp.float32
XCS = (384, 256, 384)
TILE = 192
LNB = 64


def place(x, y, z, c):
    x, y, z = x % 4, y % 4, z % 4
    return ((y * 4 + x) * 2 + z % 2, (z // 2) * 2 + c)


def where_am_i():
    q = lax.axis_index("queue")
    h = lax.axis_index("head")
    return (q // 2) % 4, q // 8, (h // 2) * 2 + q % 2, h % 2


def remote(src, dst, ss, rs, dev):
    return pltpu.make_async_remote_copy(
        src_ref=src, dst_ref=dst, send_sem=ss, recv_sem=rs, device_id=dev, device_id_type=MESH
    )


def project_kernel(
    lat, ctl, mods, wk, wv, wq, bias,
    qo, ko, vo, pko, pvo, biaso,
    W, N, lstage, cstage, acc, sq, sqr,
    stsem, plsem, plrsem, asem, arsem, bsem, brsem, fsem, frsem,
    xsem, xrsem, ssem, srsem, ksem, krsem, bisem, birsem,
    *, compute=True,
):
    x, y, z, c = where_am_i()
    zl = z % 2
    zh = z // 2
    mine = place(x, y, z, c)
    partner = place(x, y, z, 1 - c)
    swapped = c != zl
    p = y * 4 + x
    pn = (p + 1) % 16
    pp = (p + 15) % 16
    nxt = place(pn % 4, pn // 4, z, 1 - c)
    prv = place(pp % 4, pp // 4, z, 1 - c)

    barrier = pltpu.get_barrier_semaphore()

    def greet(dev):
        pl.semaphore_signal(barrier, inc=1, device_id=dev, device_id_type=MESH)

    for d in (1, 2, 3):
        greet(place(x + d, y, z, c))
        greet(place(x, y + d, z, c))
        greet(place(x, y, z + d, c))
    greet(partner)

    @pl.when(c == 1)
    def _():
        greet(nxt)

    @pl.when(c == 0)
    def _():
        greet(prv)

    @pl.when(swapped)
    def _():
        greet(place(x, y, z + 1, 1 - c))
        greet(place(x, y, z + 3, 1 - c))

    pl.semaphore_wait(barrier, jnp.where(swapped, 13, 11))

    swap_dev = place(x, y, 2 * zh + c, 1 - c)
    ws = (wk, wv, wq)

    def slot(m):
        return W.at[m, y, x, zl]

    @pl.when(swapped)
    def _():
        for m in range(3):
            remote(ws[m], slot(m), plsem.at[m], plrsem.at[m], swap_dev).start()
        remote(bias, biaso, bisem, birsem, swap_dev).start()

    @pl.when(jnp.logical_not(swapped))
    def _():
        for m in range(3):
            pltpu.make_async_copy(ws[m], slot(m), plsem.at[m]).start()
        pltpu.make_async_copy(bias, biaso, bisem).start()

    n_chunks = jnp.where(swapped, 384 // LNB, 768 // LNB)
    row0 = jnp.where(swapped, zh * 384, 0)
    out0 = jnp.where(swapped, 768, 0)

    def stage(i, s):
        r = pl.multiple_of(row0 + i * LNB, LNB)
        return (
            pltpu.make_async_copy(lat.at[pl.ds(r, LNB)], lstage.at[s], stsem.at[0, s]),
            pltpu.make_async_copy(ctl.at[pl.ds(r, LNB)], cstage.at[s], stsem.at[1, s]),
        )

    for cp in stage(0, 0):
        cp.start()

    def piece(m, half, d, part):
        rows = slice(None) if part is None else pl.ds(part * 80, 80)
        if half == 0:
            return W.at[m, y, (x + 4 - d) % 4, c, rows, pl.ds(0, XCS[m])]
        return W.at[m, (y + 4 - d) % 4, x, c, rows, pl.ds(XCS[m], 640 - XCS[m])]

    def chunk(m, half, d, part=None):
        many = slice(None) if part is None else pl.ds(part * 2, 2)
        if half == 0:
            return W.at[m, (y + 4 - d) % 4, many, c, :, pl.ds(0, XCS[m])]
        return W.at[m, many, (x + 4 - d) % 4, c, :, pl.ds(XCS[m], 640 - XCS[m])]

    def along(axis, way):
        d = 1 if way == 0 else 3
        return place(x + d, y, z, c) if axis == 0 else place(x, y + d, z, c)

    def a_copy(m, half, way, part):
        ref = piece(m, half, 0, part)
        return remote(ref, ref, asem.at[m, half, way, part], arsem.at[m, half, way, part], along(half, way))

    def a_relay(m, half, way):
        ref = piece(m, half, 1 if way == 0 else 3, way)
        return remote(ref, ref, asem.at[m, half, way, 2], arsem.at[m, half, way, 2], along(half, way))

    def b_copy(m, half, way, part):
        ref = chunk(m, half, 0, part)
        return remote(ref, ref, bsem.at[m, half, way, part], brsem.at[m, half, way, part], along(1 - half, way))

    def b_relay(m, half, way):
        ref = chunk(m, half, 1 if way == 0 else 3, way)
        return remote(ref, ref, bsem.at[m, half, way, 2], brsem.at[m, half, way, 2], along(1 - half, way))

    def f_copy(m, half, d):
        ref = chunk(m, half, d)
        return remote(ref, ref, fsem.at[m, half, d], frsem.at[m, half, d], partner)

    def step_a1(m):
        @pl.when(swapped)
        def _():
            remote(ws[m], W.at[m, y, x, c], plsem.at[m], plrsem.at[m], swap_dev).wait()

        @pl.when(jnp.logical_not(swapped))
        def _():
            pltpu.make_async_copy(ws[m], slot(m), plsem.at[m]).wait()

        for part in (0, 1):
            for way in (0, 1):
                for half in (0, 1):
                    a_copy(m, half, way, part ^ way).start()

    def step_a2(m):
        for way in (0, 1):
            for half in (0, 1):
                a_copy(m, half, way, way).wait_recv()
                a_relay(m, half, way).start()

    def step_b1(m):
        for half in (0, 1):
            for way in (0, 1):
                a_copy(m, half, way, 1 - way).wait_recv()
                a_relay(m, half, way).wait_recv()
        for part in (0, 1):
            for way in (0, 1):
                for half in (0, 1):
                    b_copy(m, half, way, part ^ way).start()
        for half in (0, 1):
            f_copy(m, half, 0).start()

    def step_b2(m):
        for way in (0, 1):
            for half in (0, 1):
                b_copy(m, half, way, way).wait_recv()
                b_relay(m, half, way).start()

    def step_f(m):
        for half in (0, 1):
            for way in (0, 1):
                b_copy(m, half, way, 1 - way).wait_recv()
                f_copy(m, half, 1 if way == 0 else 3).start()

    def step_f2(m):
        for half in (0, 1):
            for way in (0, 1):
                b_relay(m, half, way).wait_recv()
            f_copy(m, half, 2).start()

    step_a1(0)

    def x_copy(i, by):
        src = N.at[pl.ds(pl.multiple_of(768 + i * LNB, LNB), LNB)]
        dst = N.at[pl.ds(pl.multiple_of(zh * 384 + i * LNB, LNB), LNB)]
        k = 0 if by == 1 else 1
        return remote(src, dst, xsem.at[k, i], xrsem.at[zh, i], place(x, y, z + by, 1 - c))

    def ln_rows(i, s):
        span = jnp.where(swapped, zh, (i * LNB) // 384)

        def body(j, carry):
            r = pl.multiple_of(j * 16, 16)
            hid = lstage[s, pl.ds(r, 16), :].astype(F32) + cstage[s, pl.ds(r, 16), :].astype(F32)
            cen = hid - jnp.mean(hid, axis=-1, keepdims=True)
            var = jnp.mean(cen * cen, axis=-1, keepdims=True)
            nrm = cen * lax.rsqrt(var + 1e-6) * (1.0 + mods[span, 1:2, :]) + mods[span, 0:1, :]
            N[pl.ds(pl.multiple_of(out0 + i * LNB + r, 16), 16), :] = nrm.astype(BF)
            return carry

        lax.fori_loop(0, LNB // 16, body, 0)

    def ln_step(i, carry):
        s = i % 2

        @pl.when(i + 1 < n_chunks)
        def _():
            for cp in stage(i + 1, 1 - s):
                cp.start()

        for cp in stage(i, s):
            cp.wait()
        ln_rows(i, s)

        @pl.when(swapped & (i > 0))
        def _():
            x_copy(i - 1, 1).start()
            x_copy(i - 1, 3).start()

        return carry

    part_chunks = n_chunks // 6
    weave = {0: (step_a1, 1), 1: (step_a2, 0), 2: (step_a1, 2), 3: (step_b1, 0), 4: (step_a2, 1), 5: (step_a2, 2)}
    for seg in range(6):
        lax.fori_loop(seg * part_chunks, (seg + 1) * part_chunks, ln_step, 0)
        fn, m = weave[seg]
        fn(m)

    @pl.when(swapped)
    def _():
        x_copy(384 // LNB - 1, 1).start()
        x_copy(384 // LNB - 1, 3).start()

    def rows_of(r):
        return [pl.ds(pl.multiple_of(s * 384 + r * (TILE // 2), TILE // 2), TILE // 2) for s in (0, 1)]

    def lhs(r, k0, kn):
        return jnp.concatenate([N[rs, pl.ds(k0, kn)] for rs in rows_of(r)], axis=0)

    def put(m, r, cols, val, first):
        for s, rs in enumerate(rows_of(r)):
            part = val[s * (TILE // 2):(s + 1) * (TILE // 2)]
            if first:
                acc[m, rs, cols] = part
            else:
                acc[m, rs, cols] += part

    def x_dot(m, d, r, first):
        yy = (y + 4 - d) % 4
        w = W[m, yy, :, :, :, 0:XCS[m]].reshape(1280, XCS[m])
        v = jnp.dot(lhs(r, pl.multiple_of(yy * 1280, 1280), 1280), w, preferred_element_type=F32)
        put(m, r, slice(0, XCS[m]), v, first)

    def y_dot(m, xp, r, first):
        v = None
        for yy in range(4):
            w = W[m, yy, pl.ds(2 * xp, 2), :, :, XCS[m]:640].reshape(640, 640 - XCS[m])
            t = jnp.dot(lhs(r, pl.multiple_of(yy * 1280 + xp * 640, 640), 640), w, preferred_element_type=F32)
            v = t if v is None else v + t
        put(m, r, slice(XCS[m], 640), v, first)

    def shared(m, half, d):
        f_copy(m, half, d).wait_recv()

    def rows_ready(r):
        @pl.when(swapped)
        def _():
            for span in (0, 1):
                lo = r * (TILE // 2) // LNB
                hi = -(-(r + 1) * (TILE // 2) // LNB)
                prev = -(-r * (TILE // 2) // LNB)
                for i in range(max(lo, prev), hi):
                    src = N.at[pl.ds(768 + i * LNB, LNB)]
                    dst = N.at[pl.ds(span * 384 + i * LNB, LNB)]
                    remote(src, dst, xsem.at[0, i], xrsem.at[span, i], partner).wait_recv()

    seen_rows = set()
    seen_w = set()

    def task(m, rlo, rhi):
        for r in range(rlo, rhi):
            if r not in seen_rows:
                seen_rows.add(r)
                rows_ready(r)
        fresh = m not in seen_w
        seen_w.add(m)
        for kind, d in (("x", 0), ("x", 1), ("x", 3), ("y", 0), ("x", 2), ("y", 1)):
            if fresh:
                if kind == "x":
                    shared(m, 0, d)
                    if d == 2:
                        shared(m, 1, 2)
                elif d == 0:
                    for dd in (0, 1, 3):
                        shared(m, 1, dd)
            if compute:
                def body(r, carry, kind=kind, d=d):
                    if kind == "x":
                        x_dot(m, d, r, d == 0)
                    else:
                        y_dot(m, x // 2 if d == 0 else 1 - x // 2, r, d == 0)
                    return carry

                lax.fori_loop(rlo, rhi, body, 0)
            if fresh and kind == "x" and d == 0:
                step_b2(m)
                if m < 2:
                    step_b1(m + 1)
                step_f(m)
            if fresh and kind == "x" and d == 3:
                step_f2(m)

    def row_sq(m, dst):
        for t in range(6):
            v = acc[m, pl.ds(t * 128, 128), :].astype(BF).astype(F32)
            s = jnp.sum(v * v, axis=-1, keepdims=True)
            wide = jnp.broadcast_to(s, (128, 128))
            sq[dst, :, pl.ds(t * 128, 128)] = jnp.transpose(wide)[0:8, :]

    def s_copy(k, d):
        return remote(
            sq.at[k], sqr.at[k, d - 1], ssem.at[k, d - 1], srsem.at[k, d - 1], place(x, y, z + d, c)
        )

    def normalize(k, m, gain, out):
        for d in (1, 2, 3):
            s_copy(k, d).wait_recv()
        tot = sq[k] + sqr[k, 0] + sqr[k, 1] + sqr[k, 2]
        scale = lax.rsqrt(tot / 2560.0 + 1e-6)
        for t in range(6):
            col = jnp.transpose(jnp.broadcast_to(scale[0:1, t * 128:(t + 1) * 128], (128, 128)))
            rs = pl.ds(t * 128, 128)
            v = acc[m, rs, :].astype(BF).astype(F32)
            out[rs, :] = (v * col[:, 0:1] * biaso[gain:gain + 1, 0:640]).astype(BF)

    task(0, 0, 2)
    task(0, 2, 3)
    task(1, 0, 3)
    task(0, 3, 4)
    @pl.when(swapped)
    def _():
        remote(bias, biaso, bisem, birsem, swap_dev).wait()

    @pl.when(jnp.logical_not(swapped))
    def _():
        pltpu.make_async_copy(bias, biaso, bisem).wait()

    row_sq(0, 0)
    for d in (1, 3, 2):
        s_copy(0, d).start()
    task(1, 3, 4)
    for t in range(6):
        rs = pl.ds(t * 128, 128)
        vo[rs, :] = acc[1, rs, :].astype(BF)
    normalize(0, 0, 17, ko)

    def k_copy(i, dev):
        return remote((ko, vo)[i], (pko, pvo)[i], ksem.at[i], krsem.at[i], dev)

    @pl.when(c == 0)
    def _():
        for i in (0, 1):
            k_copy(i, partner).start()

    @pl.when(c == 1)
    def _():
        for i in (0, 1):
            k_copy(i, nxt).start()

    task(2, 0, 4)
    row_sq(2, 1)
    for d in (1, 3, 2):
        s_copy(1, d).start()
    normalize(1, 2, 16, qo)

    for i in (0, 1):
        k_copy(i, partner).wait_recv()
        k_copy(i, partner).wait_send()
    for k in (0, 1):
        for d in (1, 2, 3):
            s_copy(k, d).wait_send()
    for m in range(3):
        for half in (0, 1):
            for way in (0, 1):
                for part in (0, 1):
                    a_copy(m, half, way, part).wait_send()
                    b_copy(m, half, way, part).wait_send()
                a_relay(m, half, way).wait_send()
                b_relay(m, half, way).wait_send()
            for d in range(4):
                f_copy(m, half, d).wait_send()

    @pl.when(swapped)
    def _():
        for i in range(384 // LNB):
            x_copy(i, 1).wait_send()
            x_copy(i, 3).wait_send()


def project(lat, ctl, mods, wk, wv, wq, bias, compute=True):
    o = jax.ShapeDtypeStruct((768, 640), BF)
    any_ = pl.BlockSpec(memory_space=pl.ANY)
    vm = pl.BlockSpec(memory_space=pltpu.VMEM)
    D = pltpu.SemaphoreType.DMA
    return pl.pallas_call(
        functools.partial(project_kernel, compute=compute),
        out_shape=[o] * 5 + [jax.ShapeDtypeStruct((24, 1152), F32)],
        in_specs=[any_, any_, vm, any_, any_, any_, any_],
        out_specs=[vm] * 6,
        scratch_shapes=[
            pltpu.VMEM((3, 4, 4, 2, 160, 640), BF),
            pltpu.VMEM((1152, 5120), BF),
            pltpu.VMEM((2, LNB, 5120), BF),
            pltpu.VMEM((2, LNB, 5120), BF),
            pltpu.VMEM((3, 768, 640), F32),
            pltpu.VMEM((2, 8, 768), F32),
            pltpu.VMEM((2, 3, 8, 768), F32),
            D((2, 2)), D((3,)), D((3,)),
            D((3, 2, 2, 3)), D((3, 2, 2, 3)), D((3, 2, 2, 3)), D((3, 2, 2, 3)), D((3, 2, 4)), D((3, 2, 4)),
            D((2, 384 // LNB)), D((2, 384 // LNB)), D((2, 3)), D((2, 3)), D((2,)), D((2,)), D, D,
        ],
        compiler_params=pltpu.CompilerParams(
            collective_id=0, has_side_effects=True, vmem_limit_bytes=61 * 2**20
        ),
        name="project",
    )(lat, ctl, mods, wk, wv, wq, bias)


def attend_kernel(q, k, v, pk, pv, bias, out):
    for s in (0, 1):
        qs = q[s * 384:(s + 1) * 384, :]
        if s == 0:
            keys = (pk[0:384, :], pk[384:768, :], k[0:384, :])
            vals = (pv[0:384, :], pv[384:768, :], v[0:384, :])
        else:
            keys = (pk[384:768, :], k[0:384, :], k[384:768, :])
            vals = (pv[384:768, :], v[0:384, :], v[384:768, :])
        kk = jnp.concatenate(keys, axis=0)
        vv = jnp.concatenate(vals, axis=0)
        for t in range(3):
            sc = lax.dot_general(qs[t * 128:(t + 1) * 128], kk, (((1,), (1,)), ((), ())), preferred_element_type=F32)
            sc = sc * HD ** -0.5 + bias[8 * s:8 * s + 1, :]
            top = jnp.max(sc, axis=-1, keepdims=True)
            ex = jnp.exp(sc - top)
            pr = (ex * (1.0 / jnp.sum(ex, axis=-1, keepdims=True))).astype(BF)
            o = jnp.dot(pr, vv, preferred_element_type=F32)
            out[pl.ds(s * 384 + t * 128, 128), :] = o.astype(BF)


def attend(q, k, v, pk, pv, bias):
    blk = pl.BlockSpec((768, 128), lambda i: (0, i))
    return pl.pallas_call(
        attend_kernel,
        grid=(5,),
        out_shape=jax.ShapeDtypeStruct((768, 640), BF),
        in_specs=[blk] * 5 + [pl.BlockSpec((24, 1152), lambda i: (0, 0))],
        out_specs=blk,
        name="attend",
    )(q, k, v, pk, pv, bias)


def out_kernel(
    att, wo, lat, ctl, gate, out,
    WO, AT, lbuf, cbuf,
    lsem, rsem, rrsem, asem, arsem, bsem, brsem, tsem, trsem, fsem, frsem,
):
    x, y, z, c = where_am_i()
    zl = z % 2
    h = lax.axis_index("head")
    partner = place(x, y, z, 1 - c)
    mine = c == zl
    barrier = pltpu.get_barrier_semaphore()

    def greet(dev):
        pl.semaphore_signal(barrier, inc=1, device_id=dev, device_id_type=MESH)

    def swapdev(t):
        return ((h * 4 + x) * 2 + t, y)

    for d in (1, 2, 3):
        greet(place(x + d, y, z, c))
        greet(place(x, y + d, z, c))
        greet(place(x, y, z + d, c))
    greet(partner)

    @pl.when(y != h)
    def _():
        greet(swapdev(0))
        greet(swapdev(1))

    @pl.when(y == h)
    def _():
        greet(swapdev(1 - zl))

    pl.semaphore_wait(barrier, jnp.where(y != h, 12, 11))

    spot = WO.at[h, x, zl]

    @pl.when(y != h)
    def _():
        for t in (0, 1):
            remote(wo, spot, rsem.at[t], rrsem.at[zl], swapdev(t)).start()

    @pl.when(y == h)
    def _():
        pltpu.make_async_copy(wo, spot, lsem.at[0]).start()
        remote(wo, spot, rsem.at[0], rrsem.at[zl], swapdev(1 - zl)).start()

    cols = pl.ds(pl.multiple_of(h * 1280, 1280), 1280)
    stage = (
        pltpu.make_async_copy(lat.at[:, cols], lbuf, lsem.at[1]),
        pltpu.make_async_copy(ctl.at[:, cols], cbuf, lsem.at[2]),
    )
    for cp in stage:
        cp.start()

    own = AT.at[z]

    def t_copy(d):
        return remote(att, own, tsem.at[d - 1], trsem.at[d - 1], place(x, y, z + d, c))

    @pl.when(mine)
    def _():
        pltpu.make_async_copy(att, own, lsem.at[3]).start()
        t_copy(2).start()

    @pl.when(jnp.logical_not(mine))
    def _():
        t_copy(1).start()
        t_copy(3).start()

    def pc(t):
        return WO.at[y, x, t]

    @pl.when(y != h)
    def _():
        for t in (0, 1):
            remote(wo, pc(t), rsem.at[t], rrsem.at[t], partner).wait_recv()

    @pl.when(y == h)
    def _():
        pltpu.make_async_copy(wo, spot, lsem.at[0]).wait()
        remote(wo, spot, rsem.at[0], rrsem.at[1 - zl], partner).wait_recv()

    def along(axis, way):
        d = 1 if way == 0 else 3
        return place(x + d, y, z, c) if axis == 0 else place(x, y + d, z, c)

    def piece(half, d, part):
        rows = pl.ds(part * 80, 80)
        if half == 0:
            return WO.at[y, (x + 4 - d) % 4, 0, rows]
        return WO.at[(y + 4 - d) % 4, x, 1, rows]

    def chunk(half, d, part):
        many = pl.ds(part * 2, 2)
        if half == 0:
            return WO.at[(y + 4 - d) % 4, many, 0]
        return WO.at[many, (x + 4 - d) % 4, 1]

    def a_copy(half, way, part):
        ref = piece(half, 0, part)
        return remote(ref, ref, asem.at[half, way, part], arsem.at[half, way, part], along(half, way))

    def a_relay(half, way):
        ref = piece(half, 1 if way == 0 else 3, way)
        return remote(ref, ref, asem.at[half, way, 2], arsem.at[half, way, 2], along(half, way))

    def b_copy(half, way, part):
        ref = chunk(half, 0, part)
        return remote(ref, ref, bsem.at[half, way, part], brsem.at[half, way, part], along(1 - half, way))

    def b_relay(half, way):
        ref = chunk(half, 1 if way == 0 else 3, way)
        return remote(ref, ref, bsem.at[half, way, 2], brsem.at[half, way, 2], along(1 - half, way))

    every = [(half, way) for half in (0, 1) for way in (0, 1)]
    for part in (0, 1):
        for half, way in every:
            a_copy(half, way, part ^ way).start()
    for half, way in every:
        a_copy(half, way, way).wait_recv()
        a_relay(half, way).start()
    for half, way in every:
        a_copy(half, way, 1 - way).wait_recv()
        a_relay(half, way).wait_recv()
    for part in (0, 1):
        for half, way in every:
            b_copy(half, way, part ^ way).start()

    def f_copy(g):
        ref = AT.at[g]
        return remote(ref, ref, fsem.at[g], frsem.at[g], partner)

    @pl.when(mine)
    def _():
        pltpu.make_async_copy(att, own, lsem.at[3]).wait()
        f_copy(z).start()

    for half, way in every:
        b_copy(half, way, way).wait_recv()
        b_relay(half, way).start()

    @pl.when(mine)
    def _():
        for d in (1, 3, 2):
            g = (z + 4 - d) % 4
            remote(att, AT.at[g], tsem.at[d - 1], trsem.at[d - 1], partner).wait_recv()
            f_copy(g).start()

    @pl.when(jnp.logical_not(mine))
    def _():
        for g in range(4):
            f_copy(g).wait_recv()

    for half, way in every:
        b_copy(half, way, 1 - way).wait_recv()
    for half, way in every:
        b_relay(half, way).wait_recv()
    for cp in stage:
        cp.wait()

    def rows_body(r, carry):
        rs = pl.ds(pl.multiple_of(r * 128, 128), 128)
        acc = None
        for g in range(4):
            t = lax.dot_general(
                AT[g, rs, :], WO[g].reshape(1280, 640), (((1,), (1,)), ((), ())), preferred_element_type=F32
            ).astype(BF).astype(F32)
            acc = t if acc is None else acc + t
        hid = lbuf[rs, :].astype(F32) + cbuf[rs, :].astype(F32)
        out[rs, :] = hid + gate[r // 3] * acc
        return carry

    lax.fori_loop(0, 6, rows_body, 0)

    for half, way in every:
        for part in (0, 1):
            a_copy(half, way, part).wait_send()
            b_copy(half, way, part).wait_send()
        a_relay(half, way).wait_send()
        b_relay(half, way).wait_send()

    @pl.when(y != h)
    def _():
        for t in (0, 1):
            remote(wo, spot, rsem.at[t], rrsem.at[zl], swapdev(t)).wait_send()

    @pl.when(y == h)
    def _():
        remote(wo, spot, rsem.at[0], rrsem.at[zl], swapdev(1 - zl)).wait_send()

    @pl.when(mine)
    def _():
        t_copy(2).wait_send()
        for g in range(4):
            f_copy(g).wait_send()

    @pl.when(jnp.logical_not(mine))
    def _():
        t_copy(1).wait_send()
        t_copy(3).wait_send()


def out_project(att, wo, lat, ctl, gate):
    any_ = pl.BlockSpec(memory_space=pl.ANY)
    vm = pl.BlockSpec(memory_space=pltpu.VMEM)
    D = pltpu.SemaphoreType.DMA
    return pl.pallas_call(
        out_kernel,
        out_shape=jax.ShapeDtypeStruct((768, 1280), F32),
        in_specs=[any_, any_, any_, any_, vm],
        out_specs=vm,
        scratch_shapes=[
            pltpu.VMEM((4, 4, 2, 160, 640), BF),
            pltpu.VMEM((4, 768, 640), BF),
            pltpu.VMEM((768, 1280), BF),
            pltpu.VMEM((768, 1280), BF),
            D((4,)), D((2,)), D((2,)),
            D((2, 2, 3)), D((2, 2, 3)), D((2, 2, 3)), D((2, 2, 3)),
            D((3,)), D((3,)), D((4,)), D((4,)),
        ],
        compiler_params=pltpu.CompilerParams(
            collective_id=1, has_side_effects=True, vmem_limit_bytes=40 * 2**20
        ),
        name="out_project",
    )(att, wo, lat, ctl, gate)


def shards(latents, control, levels, window_mask, modulation, w_query, w_key, w_value, w_out, q_gain, k_gain):
    owner = lax.axis_index("queue")
    head = lax.axis_index("head")
    lat = latents.reshape(768, 5120)
    ctl = control.reshape(768, 5120)
    mods = jnp.stack([lax.dynamic_index_in_dim(modulation, levels[s], 0, keepdims=False) for s in (0, 1)])
    gate = lax.dynamic_slice_in_dim(mods[:, 2:3], head * 1280, 1280, 2)
    ids = owner * 2 + jnp.arange(2, dtype=jnp.int32)
    seen = jnp.stack(
        [(window_mask[:, 0] == 1) & (ids >= 2), (window_mask[:, 1] == 1) & (ids >= 1), jnp.ones((2,), dtype=bool)],
        axis=1,
    )
    bias = jnp.where(jnp.repeat(seen, 384, axis=1), 0.0, -1e30).astype(F32)
    bias = jnp.broadcast_to(bias[:, None, :], (2, 8, 1152)).reshape(16, 1152)
    gains = jnp.pad(jnp.stack([q_gain, k_gain]), ((0, 6), (0, 512)))
    bias = jnp.concatenate([bias, gains], axis=0)
    q, k, v, pk, pv, bias = project(
        lat, ctl, mods[:, 0:2], w_key, w_value, w_query, bias
    )
    att = attend(q, k, v, pk, pv, bias)
    updated = out_project(att, w_out.T, lat, ctl, gate)
    pairs = [(i, (i + 1) % 32) for i in range(32)]
    last = lax.ppermute(updated[384:].astype(BF), "queue", pairs).astype(F32)
    return jnp.stack([last, updated[:384]])


def solution(mesh):
    placed = (
        P("queue", None, None),
        P("queue", None, None),
        P("queue"),
        P("queue", None),
        P(),
        P("queue", "head"),
        P("queue", "head"),
        P("queue", "head"),
        P("head", "queue"),
        P("head"),
        P("head"),
    )
    return jax.shard_map(
        shards, mesh=mesh, in_specs=placed, out_specs=P("queue", None, "head"), check_vma=False
    )
```

```python
import functools

import jax
import jax.numpy as jnp
from jax import lax
from jax.experimental import pallas as pl
from jax.experimental.pallas import tpu as pltpu
from jax.sharding import PartitionSpec as P

HD = 128
MESH = pl.DeviceIdType.MESH
BF = jnp.bfloat16
F32 = jnp.float32
XCS = (384, 256, 384)
TILE = 192
LNB = 64


def place(x, y, z, c):
    x, y, z = x % 4, y % 4, z % 4
    return ((y * 4 + x) * 2 + z % 2, (z // 2) * 2 + c)


def where_am_i():
    q = lax.axis_index("queue")
    h = lax.axis_index("head")
    return (q // 2) % 4, q // 8, (h // 2) * 2 + q % 2, h % 2


def remote(src, dst, ss, rs, dev):
    return pltpu.make_async_remote_copy(
        src_ref=src, dst_ref=dst, send_sem=ss, recv_sem=rs, device_id=dev, device_id_type=MESH
    )


def block_kernel(
    lat, ctl, mods, wk, wv, wq, bias, wo, gate,
    out,
    W, N, lstage, cstage, acc, sq, sqr, qo, ko, vo, pko, pvo, biaso, WO, AT, shout, shin,
    stsem, plsem, plrsem, asem, arsem, bsem, brsem, fsem, frsem,
    xsem, xrsem, ssem, srsem, ksem, krsem, bisem, birsem,
    rsem, rrsem, wasem, warsem, wbsem, wbrsem, tsem, trsem, gsem, grsem, lsem, hsem, hrsem,
):
    x, y, z, c = where_am_i()
    zl = z % 2
    zh = z // 2
    mine = place(x, y, z, c)
    partner = place(x, y, z, 1 - c)
    swapped = c != zl
    p = y * 4 + x
    pn = (p + 1) % 16
    pp = (p + 15) % 16
    nxt = place(pn % 4, pn // 4, z, 1 - c)
    prv = place(pp % 4, pp // 4, z, 1 - c)

    q = lax.axis_index("queue")
    h = lax.axis_index("head")
    after = ((q + 1) % 32, h)
    before = ((q + 31) % 32, h)
    barrier = pltpu.get_barrier_semaphore()

    def swapdev(t):
        return ((h * 4 + x) * 2 + t, y)


    def greet(dev):
        pl.semaphore_signal(barrier, inc=1, device_id=dev, device_id_type=MESH)

    for d in (1, 2, 3):
        greet(place(x + d, y, z, c))
        greet(place(x, y + d, z, c))
        greet(place(x, y, z + d, c))
    greet(partner)

    @pl.when(c == 1)
    def _():
        greet(nxt)

    @pl.when(c == 0)
    def _():
        greet(prv)

    @pl.when(swapped)
    def _():
        greet(place(x, y, z + 1, 1 - c))
        greet(place(x, y, z + 3, 1 - c))

    @pl.when(y != h)
    def _():
        greet(swapdev(0))
        greet(swapdev(1))

    @pl.when(y == h)
    def _():
        greet(swapdev(1 - zl))

    greet(after)
    greet(before)
    pl.semaphore_wait(barrier, jnp.where(swapped, 13, 11) + jnp.where(y != h, 2, 1) + 2)

    swap_dev = place(x, y, 2 * zh + c, 1 - c)
    ws = (wk, wv, wq)

    def slot(m):
        return W.at[m, y, x, zl]

    @pl.when(swapped)
    def _():
        for m in range(3):
            remote(ws[m], slot(m), plsem.at[m], plrsem.at[m], swap_dev).start()
        remote(bias, biaso, bisem, birsem, swap_dev).start()

    @pl.when(jnp.logical_not(swapped))
    def _():
        for m in range(3):
            pltpu.make_async_copy(ws[m], slot(m), plsem.at[m]).start()
        pltpu.make_async_copy(bias, biaso, bisem).start()

    n_chunks = jnp.where(swapped, 384 // LNB, 768 // LNB)
    row0 = jnp.where(swapped, zh * 384, 0)
    out0 = jnp.where(swapped, 768, 0)

    def stage(i, s):
        r = pl.multiple_of(row0 + i * LNB, LNB)
        return (
            pltpu.make_async_copy(lat.at[pl.ds(r, LNB)], lstage.at[s], stsem.at[0, s]),
            pltpu.make_async_copy(ctl.at[pl.ds(r, LNB)], cstage.at[s], stsem.at[1, s]),
        )

    for cp in stage(0, 0):
        cp.start()

    def piece(m, half, d, part):
        rows = slice(None) if part is None else pl.ds(part * 80, 80)
        if half == 0:
            return W.at[m, y, (x + 4 - d) % 4, c, rows, pl.ds(0, XCS[m])]
        return W.at[m, (y + 4 - d) % 4, x, c, rows, pl.ds(XCS[m], 640 - XCS[m])]

    def chunk(m, half, d, part=None):
        many = slice(None) if part is None else pl.ds(part * 2, 2)
        if half == 0:
            return W.at[m, (y + 4 - d) % 4, many, c, :, pl.ds(0, XCS[m])]
        return W.at[m, many, (x + 4 - d) % 4, c, :, pl.ds(XCS[m], 640 - XCS[m])]

    def along(axis, way):
        d = 1 if way == 0 else 3
        return place(x + d, y, z, c) if axis == 0 else place(x, y + d, z, c)

    def a_copy(m, half, way, part):
        ref = piece(m, half, 0, part)
        return remote(ref, ref, asem.at[m, half, way, part], arsem.at[m, half, way, part], along(half, way))

    def a_relay(m, half, way):
        ref = piece(m, half, 1 if way == 0 else 3, way)
        return remote(ref, ref, asem.at[m, half, way, 2], arsem.at[m, half, way, 2], along(half, way))

    def b_copy(m, half, way, part):
        ref = chunk(m, half, 0, part)
        return remote(ref, ref, bsem.at[m, half, way, part], brsem.at[m, half, way, part], along(1 - half, way))

    def b_relay(m, half, way):
        ref = chunk(m, half, 1 if way == 0 else 3, way)
        return remote(ref, ref, bsem.at[m, half, way, 2], brsem.at[m, half, way, 2], along(1 - half, way))

    def f_copy(m, half, d):
        ref = chunk(m, half, d)
        return remote(ref, ref, fsem.at[m, half, d], frsem.at[m, half, d], partner)

    def step_a1(m):
        @pl.when(swapped)
        def _():
            remote(ws[m], W.at[m, y, x, c], plsem.at[m], plrsem.at[m], swap_dev).wait()

        @pl.when(jnp.logical_not(swapped))
        def _():
            pltpu.make_async_copy(ws[m], slot(m), plsem.at[m]).wait()

        for part in (0, 1):
            for way in (0, 1):
                for half in (0, 1):
                    a_copy(m, half, way, part ^ way).start()

    def step_a2(m):
        for way in (0, 1):
            for half in (0, 1):
                a_copy(m, half, way, way).wait_recv()
                a_relay(m, half, way).start()

    def step_b1(m):
        for half in (0, 1):
            for way in (0, 1):
                a_copy(m, half, way, 1 - way).wait_recv()
                a_relay(m, half, way).wait_recv()
        for part in (0, 1):
            for way in (0, 1):
                for half in (0, 1):
                    b_copy(m, half, way, part ^ way).start()
        for half in (0, 1):
            f_copy(m, half, 0).start()

    def step_b2(m):
        for way in (0, 1):
            for half in (0, 1):
                b_copy(m, half, way, way).wait_recv()
                b_relay(m, half, way).start()

    def step_f(m):
        for half in (0, 1):
            for way in (0, 1):
                b_copy(m, half, way, 1 - way).wait_recv()
                f_copy(m, half, 1 if way == 0 else 3).start()

    def step_f2(m):
        for half in (0, 1):
            for way in (0, 1):
                b_relay(m, half, way).wait_recv()
            f_copy(m, half, 2).start()

    step_a1(0)

    def x_copy(i, by):
        src = N.at[pl.ds(pl.multiple_of(768 + i * LNB, LNB), LNB)]
        dst = N.at[pl.ds(pl.multiple_of(zh * 384 + i * LNB, LNB), LNB)]
        k = 0 if by == 1 else 1
        return remote(src, dst, xsem.at[k, i], xrsem.at[zh, i], place(x, y, z + by, 1 - c))

    def ln_rows(i, s):
        span = jnp.where(swapped, zh, (i * LNB) // 384)

        def body(j, carry):
            r = pl.multiple_of(j * 16, 16)
            hid = lstage[s, pl.ds(r, 16), :].astype(F32) + cstage[s, pl.ds(r, 16), :].astype(F32)
            cen = hid - jnp.mean(hid, axis=-1, keepdims=True)
            var = jnp.mean(cen * cen, axis=-1, keepdims=True)
            nrm = cen * lax.rsqrt(var + 1e-6) * (1.0 + mods[span, 1:2, :]) + mods[span, 0:1, :]
            N[pl.ds(pl.multiple_of(out0 + i * LNB + r, 16), 16), :] = nrm.astype(BF)
            return carry

        lax.fori_loop(0, LNB // 16, body, 0)

    def ln_step(i, carry):
        s = i % 2

        @pl.when(i + 1 < n_chunks)
        def _():
            for cp in stage(i + 1, 1 - s):
                cp.start()

        for cp in stage(i, s):
            cp.wait()
        ln_rows(i, s)

        @pl.when(swapped & (i > 0))
        def _():
            x_copy(i - 1, 1).start()
            x_copy(i - 1, 3).start()

        return carry

    part_chunks = n_chunks // 6
    weave = {0: (step_a1, 1), 1: (step_a2, 0), 2: (step_a1, 2), 3: (step_b1, 0), 4: (step_a2, 1), 5: (step_a2, 2)}
    for seg in range(6):
        lax.fori_loop(seg * part_chunks, (seg + 1) * part_chunks, ln_step, 0)
        fn, m = weave[seg]
        fn(m)

    @pl.when(swapped)
    def _():
        x_copy(384 // LNB - 1, 1).start()
        x_copy(384 // LNB - 1, 3).start()

    def rows_of(r):
        return [pl.ds(pl.multiple_of(s * 384 + r * (TILE // 2), TILE // 2), TILE // 2) for s in (0, 1)]

    def lhs(r, k0, kn):
        return jnp.concatenate([N[rs, pl.ds(k0, kn)] for rs in rows_of(r)], axis=0)

    def put(m, r, cols, val, first):
        for s, rs in enumerate(rows_of(r)):
            part = val[s * (TILE // 2):(s + 1) * (TILE // 2)]
            if first:
                acc[m, rs, cols] = part
            else:
                acc[m, rs, cols] += part

    def x_dot(m, d, r, first):
        yy = (y + 4 - d) % 4
        w = W[m, yy, :, :, :, 0:XCS[m]].reshape(1280, XCS[m])
        v = jnp.dot(lhs(r, pl.multiple_of(yy * 1280, 1280), 1280), w, preferred_element_type=F32)
        put(m, r, slice(0, XCS[m]), v, first)

    def y_dot(m, xp, r, first):
        v = None
        for yy in range(4):
            w = W[m, yy, pl.ds(2 * xp, 2), :, :, XCS[m]:640].reshape(640, 640 - XCS[m])
            t = jnp.dot(lhs(r, pl.multiple_of(yy * 1280 + xp * 640, 640), 640), w, preferred_element_type=F32)
            v = t if v is None else v + t
        put(m, r, slice(XCS[m], 640), v, first)

    def shared(m, half, d):
        f_copy(m, half, d).wait_recv()

    def rows_ready(r):
        @pl.when(swapped)
        def _():
            for span in (0, 1):
                lo = r * (TILE // 2) // LNB
                hi = -(-(r + 1) * (TILE // 2) // LNB)
                prev = -(-r * (TILE // 2) // LNB)
                for i in range(max(lo, prev), hi):
                    src = N.at[pl.ds(768 + i * LNB, LNB)]
                    dst = N.at[pl.ds(span * 384 + i * LNB, LNB)]
                    remote(src, dst, xsem.at[0, i], xrsem.at[span, i], partner).wait_recv()

    def row_sq(m, dst):
        for t in range(6):
            v = acc[m, pl.ds(t * 128, 128), :].astype(BF).astype(F32)
            s = jnp.sum(v * v, axis=-1, keepdims=True)
            wide = jnp.broadcast_to(s, (128, 128))
            sq[dst, :, pl.ds(t * 128, 128)] = jnp.transpose(wide)[0:8, :]

    def s_copy(k, d):
        return remote(
            sq.at[k], sqr.at[k, d - 1], ssem.at[k, d - 1], srsem.at[k, d - 1], place(x, y, z + d, c)
        )

    def normalize(k, m, gain, out):
        for d in (1, 2, 3):
            s_copy(k, d).wait_recv()
        tot = sq[k] + sqr[k, 0] + sqr[k, 1] + sqr[k, 2]
        scale = lax.rsqrt(tot / 2560.0 + 1e-6)
        for t in range(6):
            col = jnp.transpose(jnp.broadcast_to(scale[0:1, t * 128:(t + 1) * 128], (128, 128)))
            rs = pl.ds(t * 128, 128)
            v = acc[m, rs, :].astype(BF).astype(F32)
            out[rs, :] = (v * col[:, 0:1] * biaso[gain:gain + 1, 0:640]).astype(BF)

    def steps(m, kinds, rlo, rhi, fresh):
        for kind, d in kinds:
            if fresh:
                if kind == "x":
                    shared(m, 0, d)
                elif d == 0:
                    for dd in (0, 1, 3):
                        shared(m, 1, dd)
                else:
                    shared(m, 1, 2)

            def body(r, carry, kind=kind, d=d):
                if kind == "x":
                    x_dot(m, d, r, d == 0)
                else:
                    y_dot(m, x // 2 if d == 0 else 1 - x // 2, r, d == 0)
                return carry

            lax.fori_loop(rlo, rhi, body, 0)

    early = (("x", 0), ("x", 1), ("x", 3), ("y", 0))
    late = (("x", 2), ("y", 1))

    spot = WO.at[h, x, zl]

    def w_place():
        @pl.when(y != h)
        def _():
            for t in (0, 1):
                remote(wo, spot, rsem.at[t], rrsem.at[zl], swapdev(t)).start()

        @pl.when(y == h)
        def _():
            pltpu.make_async_copy(wo, spot, lsem.at[0]).start()
            remote(wo, spot, rsem.at[0], rrsem.at[zl], swapdev(1 - zl)).start()

    def w_placed():
        @pl.when(y != h)
        def _():
            for t in (0, 1):
                remote(wo, WO.at[y, x, t], rsem.at[t], rrsem.at[t], partner).wait_recv()

        @pl.when(y == h)
        def _():
            pltpu.make_async_copy(wo, spot, lsem.at[0]).wait()
            remote(wo, spot, rsem.at[0], rrsem.at[1 - zl], partner).wait_recv()

    def w_piece(half, d, part):
        rows = pl.ds(part * 80, 80)
        if half == 0:
            return WO.at[y, (x + 4 - d) % 4, 0, rows]
        return WO.at[(y + 4 - d) % 4, x, 1, rows]

    def w_chunk(half, d, part):
        many = pl.ds(part * 2, 2)
        if half == 0:
            return WO.at[(y + 4 - d) % 4, many, 0]
        return WO.at[many, (x + 4 - d) % 4, 1]

    def wa_copy(half, way, part):
        ref = w_piece(half, 0, part)
        return remote(ref, ref, wasem.at[half, way, part], warsem.at[half, way, part], along(half, way))

    def wa_relay(half, way):
        ref = w_piece(half, 1 if way == 0 else 3, way)
        return remote(ref, ref, wasem.at[half, way, 2], warsem.at[half, way, 2], along(half, way))

    def wb_copy(half, way, part):
        ref = w_chunk(half, 0, part)
        return remote(ref, ref, wbsem.at[half, way, part], wbrsem.at[half, way, part], along(1 - half, way))

    def wb_relay(half, way):
        ref = w_chunk(half, 1 if way == 0 else 3, way)
        return remote(ref, ref, wbsem.at[half, way, 2], wbrsem.at[half, way, 2], along(1 - half, way))

    every = [(half, way) for way in (0, 1) for half in (0, 1)]

    def w_a1():
        w_placed()
        for part in (0, 1):
            for half, way in every:
                wa_copy(half, way, part ^ way).start()

    def w_a2():
        for half, way in every:
            wa_copy(half, way, way).wait_recv()
            wa_relay(half, way).start()

    def w_b1():
        for half, way in every:
            wa_copy(half, way, 1 - way).wait_recv()
            wa_relay(half, way).wait_recv()
        for part in (0, 1):
            for half, way in every:
                wb_copy(half, way, part ^ way).start()

    def w_b2():
        for half, way in every:
            wb_copy(half, way, way).wait_recv()
            wb_relay(half, way).start()

    def w_done():
        for half, way in every:
            wb_copy(half, way, 1 - way).wait_recv()
        for half, way in every:
            wb_relay(half, way).wait_recv()

    def head_cols(i):
        return pl.ds(i * HD, HD)

    def k_copy(t, i, dev):
        return remote(
            (ko, vo)[t].at[:, head_cols(i)], (pko, pvo)[t].at[:, head_cols(i)], ksem.at[t, i], krsem.at[t, i], dev
        )

    w_place()
    step_b2(0)
    step_b1(1)
    step_f(0)
    step_f2(0)
    rows_ready(0)
    rows_ready(1)
    steps(0, early + late, 0, 2, True)
    step_b2(1)
    step_b1(2)
    step_f(1)
    rows_ready(2)
    steps(0, early + late, 2, 3, False)
    step_f2(1)
    steps(1, early + late, 0, 3, True)
    step_b2(2)
    step_f(2)
    w_a1()
    rows_ready(3)
    steps(0, early + late, 3, 4, False)

    @pl.when(swapped)
    def _():
        remote(bias, biaso, bisem, birsem, swap_dev).wait()

    @pl.when(jnp.logical_not(swapped))
    def _():
        pltpu.make_async_copy(bias, biaso, bisem).wait()

    row_sq(0, 0)
    for d in (1, 3, 2):
        s_copy(0, d).start()
    steps(1, early + late, 3, 4, False)
    for t in range(6):
        rs = pl.ds(t * 128, 128)
        vo[rs, :] = acc[1, rs, :].astype(BF)
    normalize(0, 0, 17, ko)
    w_a2()

    for i in range(5):
        @pl.when(c == 0)
        def _():
            for t in (0, 1):
                k_copy(t, i, partner).start()

        @pl.when(c == 1)
        def _():
            for t in (0, 1):
                k_copy(t, i, nxt).start()

    steps(2, early, 0, 4, True)
    w_b1()
    step_f2(2)
    steps(2, late, 0, 4, True)
    row_sq(2, 1)
    for d in (1, 3, 2):
        s_copy(1, d).start()
    normalize(1, 2, 16, qo)

    cols = pl.ds(pl.multiple_of(h * 1280, 1280), 1280)
    resid = (
        pltpu.make_async_copy(lat.at[:, cols], N.at[pl.ds(0, 768), pl.ds(0, 1280)], lsem.at[1]),
        pltpu.make_async_copy(ctl.at[:, cols], N.at[pl.ds(0, 768), pl.ds(1280, 1280)], lsem.at[2]),
    )
    for cp in resid:
        cp.start()

    mine = c == zl
    fold = HD ** -0.5 * 1.4426950408889634

    def attend_head(i):
        cs = head_cols(i)

        def tile(t, carry):
            s = t // 3
            rs = pl.ds(pl.multiple_of(t * 128, 128), 128)
            qt = qo[rs, cs]
            prior = pl.ds(pl.multiple_of(384 * (1 - s), 384), 384)
            here = pl.ds(pl.multiple_of(384 * s, 384), 384)
            far_k, far_v = pko[here, cs], pvo[here, cs]
            own_k, own_v = ko[here, cs], vo[here, cs]
            near_k = jnp.where(s == 0, pko[pl.ds(384, 384), cs], ko[pl.ds(0, 384), cs])
            near_v = jnp.where(s == 0, pvo[pl.ds(384, 384), cs], vo[pl.ds(0, 384), cs])
            blocks = []
            for kk in (far_k, near_k, own_k):
                blocks.append(lax.dot_general(qt, kk, (((1,), (1,)), ((), ())), preferred_element_type=F32))
            bs = [biaso[pl.ds(pl.multiple_of(8 * s, 8), 8), :][0:1, b * 384:b * 384 + 1] for b in range(3)]
            tops = [jnp.max(sc, axis=-1, keepdims=True) + bv for sc, bv in zip(blocks, bs)]
            top = jnp.maximum(jnp.maximum(tops[0], tops[1]), tops[2])
            total = None
            o = None
            for sc, bv, vv in zip(blocks, bs, (far_v, near_v, own_v)):
                ex = jnp.exp2((sc - (top - bv)) * fold)
                part = jnp.sum(ex, axis=-1, keepdims=True)
                pv = jnp.dot(ex.astype(BF), vv, preferred_element_type=F32)
                total = part if total is None else total + part
                o = pv if o is None else o + pv
            qo[rs, cs] = (o * (1.0 / total)).astype(BF)
            return carry

        lax.fori_loop(0, 6, tile, 0)

    def t_copy(d, i):
        src = qo.at[:, head_cols(i)]
        return remote(src, AT.at[z, :, head_cols(i)], tsem.at[d - 1, i], trsem.at[d - 1, i], place(x, y, z + d, c))

    def own_copy(i):
        return pltpu.make_async_copy(qo.at[:, head_cols(i)], AT.at[z, :, head_cols(i)], lsem.at[4 + i])

    def g_own(i):
        return remote(qo.at[:, head_cols(i)], AT.at[z, :, head_cols(i)], gsem.at[z, i], grsem.at[z, i], partner)

    def g_copy(g, i):
        ref = AT.at[g, :, head_cols(i)]
        return remote(ref, ref, gsem.at[g, i], grsem.at[g, i], partner)

    def send_head(i):
        @pl.when(mine)
        def _():
            t_copy(2, i).start()
            own_copy(i).start()
            g_own(i).start()

        @pl.when(jnp.logical_not(mine))
        def _():
            t_copy(1, i).start()
            t_copy(3, i).start()

    def pass_head(i):
        @pl.when(mine)
        def _():
            for d in (1, 3, 2):
                g = (z + 4 - d) % 4
                t_copy(d, i).wait_recv()
                g_copy(g, i).start()

    for i in range(5):
        for t in (0, 1):
            k_copy(t, i, partner).wait_recv()
        attend_head(i)
        send_head(i)
        if i == 1:
            w_b2()
        if i >= 2:
            pass_head(i - 2)
    pass_head(3)
    pass_head(4)

    @pl.when(mine)
    def _():
        for i in range(5):
            own_copy(i).wait()

    @pl.when(jnp.logical_not(mine))
    def _():
        for i in range(5):
            for g in range(4):
                g_copy(g, i).wait_recv()

    w_done()
    for cp in resid:
        cp.wait()

    def project_rows(r):
        rs = pl.ds(pl.multiple_of(r * 128, 128), 128)
        tot = None
        for g in range(4):
            t = lax.dot_general(
                AT[g, rs, :], WO[g].reshape(1280, 640), (((1,), (1,)), ((), ())), preferred_element_type=F32
            ).astype(BF).astype(F32)
            tot = t if tot is None else tot + t
        hid = N[rs, 0:1280].astype(F32) + N[rs, 1280:2560].astype(F32)
        return hid + gate[r // 3] * tot

    def h_copy(t):
        rs = pl.ds(pl.multiple_of(t * 128, 128), 128)
        return remote(shout.at[rs], shin.at[rs], hsem.at[t], hrsem.at[t], after)

    def odd_rows(t, carry):
        shout[pl.ds(pl.multiple_of(t * 128, 128), 128), :] = project_rows(t + 3).astype(BF)

        @pl.when(t > 0)
        def _():
            h_copy(t - 1).start()

        return carry

    lax.fori_loop(0, 3, odd_rows, 0)

    def even_rows(t, carry):
        out[1, pl.ds(pl.multiple_of(t * 128, 128), 128), :] = project_rows(t)

        @pl.when(t == 0)
        def _():
            h_copy(2).start()

        return carry

    lax.fori_loop(0, 3, even_rows, 0)
    for t in range(3):
        rs = pl.ds(t * 128, 128)
        h_copy(t).wait_recv()
        out[0, rs, :] = shin[rs, :].astype(F32)

    for t in range(3):
        h_copy(t).wait_send()
    for t in (0, 1):
        for i in range(5):
            k_copy(t, i, partner).wait_send()
    for k in (0, 1):
        for d in (1, 2, 3):
            s_copy(k, d).wait_send()
    for m in range(3):
        for half in (0, 1):
            for way in (0, 1):
                for part in (0, 1):
                    a_copy(m, half, way, part).wait_send()
                    b_copy(m, half, way, part).wait_send()
                a_relay(m, half, way).wait_send()
                b_relay(m, half, way).wait_send()
            for d in range(4):
                f_copy(m, half, d).wait_send()

    @pl.when(swapped)
    def _():
        for i in range(384 // LNB):
            x_copy(i, 1).wait_send()
            x_copy(i, 3).wait_send()

    for half, way in every:
        for part in (0, 1):
            wa_copy(half, way, part).wait_send()
            wb_copy(half, way, part).wait_send()
        wa_relay(half, way).wait_send()
        wb_relay(half, way).wait_send()

    @pl.when(y != h)
    def _():
        for t in (0, 1):
            remote(wo, spot, rsem.at[t], rrsem.at[zl], swapdev(t)).wait_send()

    @pl.when(y == h)
    def _():
        remote(wo, spot, rsem.at[0], rrsem.at[zl], swapdev(1 - zl)).wait_send()

    @pl.when(mine)
    def _():
        for i in range(5):
            t_copy(2, i).wait_send()
            g_own(i).wait_send()
            for d in (1, 2, 3):
                g_copy((z + 4 - d) % 4, i).wait_send()

    @pl.when(jnp.logical_not(mine))
    def _():
        for i in range(5):
            t_copy(1, i).wait_send()
            t_copy(3, i).wait_send()


def block(lat, ctl, mods, wk, wv, wq, bias, wo, gate):
    any_ = pl.BlockSpec(memory_space=pl.ANY)
    vm = pl.BlockSpec(memory_space=pltpu.VMEM)
    D = pltpu.SemaphoreType.DMA
    rows = pltpu.VMEM((768, 640), BF)
    stage2 = D((3, 2, 2, 3))
    return pl.pallas_call(
        block_kernel,
        out_shape=jax.ShapeDtypeStruct((2, 384, 1280), F32),
        in_specs=[any_, any_, vm, any_, any_, any_, any_, any_, vm],
        out_specs=vm,
        scratch_shapes=[
            pltpu.VMEM((3, 4, 4, 2, 160, 640), BF),
            pltpu.VMEM((1152, 5120), BF),
            pltpu.VMEM((2, LNB, 5120), BF),
            pltpu.VMEM((2, LNB, 5120), BF),
            pltpu.VMEM((3, 768, 640), F32),
            pltpu.VMEM((2, 8, 768), F32),
            pltpu.VMEM((2, 3, 8, 768), F32),
            rows, rows, rows, rows, rows,
            pltpu.VMEM((24, 1152), F32),
            pltpu.VMEM((4, 4, 2, 160, 640), BF),
            pltpu.VMEM((4, 768, 640), BF),
            pltpu.VMEM((384, 1280), BF),
            pltpu.VMEM((384, 1280), BF),
            D((2, 2)), D((3,)), D((3,)),
            stage2, stage2, stage2, stage2, D((3, 2, 4)), D((3, 2, 4)),
            D((2, 384 // LNB)), D((2, 384 // LNB)), D((2, 3)), D((2, 3)), D((2, 5)), D((2, 5)), D, D,
            D((2,)), D((2,)), D((2, 2, 3)), D((2, 2, 3)), D((2, 2, 3)), D((2, 2, 3)),
            D((3, 5)), D((3, 5)), D((4, 5)), D((4, 5)), D((9,)), D((3,)), D((3,)),
        ],
        compiler_params=pltpu.CompilerParams(
            collective_id=0, has_side_effects=True, vmem_limit_bytes=67043328
        ),
        name="block",
    )(lat, ctl, mods, wk, wv, wq, bias, wo, gate)


def shards(latents, control, levels, window_mask, modulation, w_query, w_key, w_value, w_out, q_gain, k_gain):
    owner = lax.axis_index("queue")
    head = lax.axis_index("head")
    lat = latents.reshape(768, 5120)
    ctl = control.reshape(768, 5120)
    mods = jnp.stack([lax.dynamic_index_in_dim(modulation, levels[s], 0, keepdims=False) for s in (0, 1)])
    gate = lax.dynamic_slice_in_dim(mods[:, 2:3], head * 1280, 1280, 2)
    ids = owner * 2 + jnp.arange(2, dtype=jnp.int32)
    seen = jnp.stack(
        [(window_mask[:, 0] == 1) & (ids >= 2), (window_mask[:, 1] == 1) & (ids >= 1), jnp.ones((2,), dtype=bool)],
        axis=1,
    )
    bias = jnp.where(jnp.repeat(seen, 384, axis=1), 0.0, -1e30).astype(F32)
    bias = jnp.broadcast_to(bias[:, None, :], (2, 8, 1152)).reshape(16, 1152)
    gains = jnp.pad(jnp.stack([q_gain, k_gain]), ((0, 6), (0, 512)))
    bias = jnp.concatenate([bias, gains], axis=0)
    return block(lat, ctl, mods[:, 0:2], w_key, w_value, w_query, bias, w_out.T, gate)


def solution(mesh):
    placed = (
        P("queue", None, None),
        P("queue", None, None),
        P("queue"),
        P("queue", None),
        P(),
        P("queue", "head"),
        P("queue", "head"),
        P("queue", "head"),
        P("head", "queue"),
        P("head"),
        P("head"),
    )
    return jax.shard_map(
        shards, mesh=mesh, in_specs=placed, out_specs=P("queue", None, "head"), check_vma=False
    )
```

```python
import functools

import jax
import jax.numpy as jnp
from jax import lax
from jax.experimental import pallas as pl
from jax.experimental.pallas import tpu as pltpu
from jax.sharding import PartitionSpec as P

HD = 128
MESH = pl.DeviceIdType.MESH
BF = jnp.bfloat16
F32 = jnp.float32
XCS = (384, 256, 384)
TILE = 192
LNB = 64


def place(x, y, z, c):
    x, y, z = x % 4, y % 4, z % 4
    return ((y * 4 + x) * 2 + z % 2, (z // 2) * 2 + c)


def where_am_i():
    q = lax.axis_index("queue")
    h = lax.axis_index("head")
    return (q // 2) % 4, q // 8, (h // 2) * 2 + q % 2, h % 2


def remote(src, dst, ss, rs, dev):
    return pltpu.make_async_remote_copy(
        src_ref=src, dst_ref=dst, send_sem=ss, recv_sem=rs, device_id=dev, device_id_type=MESH
    )


def block_kernel(
    lat, ctl, mods, wk, wv, wq, bias, wo,
    out, shin,
    W, N, lstage, cstage, acc, sq, sqr, qo, ko, vo, pko, pvo, biaso, WO, AT, shout, EX,
    stsem, plsem, plrsem, asem, arsem, bsem, brsem, fsem, frsem,
    xsem, xrsem, ssem, srsem, ksem, krsem, bisem, birsem,
    rsem, rrsem, wasem, warsem, wbsem, wbrsem, tsem, trsem, gsem, grsem, lsem, hsem, hrsem, osem,
):
    x, y, z, c = where_am_i()
    zl = z % 2
    zh = z // 2
    mine = place(x, y, z, c)
    partner = place(x, y, z, 1 - c)
    swapped = c != zl
    p = y * 4 + x
    pn = (p + 1) % 16
    pp = (p + 15) % 16
    nxt = place(pn % 4, pn // 4, z, 1 - c)
    prv = place(pp % 4, pp // 4, z, 1 - c)

    q = lax.axis_index("queue")
    h = lax.axis_index("head")
    after = ((q + 1) % 32, h)
    before = ((q + 31) % 32, h)
    barrier = pltpu.get_barrier_semaphore()

    def swapdev(t):
        return ((h * 4 + x) * 2 + t, y)


    def greet(dev):
        pl.semaphore_signal(barrier, inc=1, device_id=dev, device_id_type=MESH)

    for d in (1, 2, 3):
        greet(place(x + d, y, z, c))
        greet(place(x, y + d, z, c))
        greet(place(x, y, z + d, c))
    greet(partner)

    @pl.when(c == 1)
    def _():
        greet(nxt)

    @pl.when(c == 0)
    def _():
        greet(prv)

    @pl.when(swapped)
    def _():
        greet(place(x, y, z + 1, 1 - c))
        greet(place(x, y, z + 3, 1 - c))

    @pl.when(y != h)
    def _():
        greet(swapdev(0))
        greet(swapdev(1))

    @pl.when(y == h)
    def _():
        greet(swapdev(1 - zl))

    greet(after)
    greet(before)
    pl.semaphore_wait(barrier, jnp.where(swapped, 13, 11) + jnp.where(y != h, 2, 1) + 2)

    swap_dev = place(x, y, 2 * zh + c, 1 - c)
    ws = (wk, wv, wq)

    def slot(m):
        return W.at[m, y, x, zl]

    @pl.when(swapped)
    def _():
        for m in range(3):
            remote(ws[m], slot(m), plsem.at[m], plrsem.at[m], swap_dev).start()
        remote(bias, biaso, bisem, birsem, swap_dev).start()

    @pl.when(jnp.logical_not(swapped))
    def _():
        for m in range(3):
            pltpu.make_async_copy(ws[m], slot(m), plsem.at[m]).start()
        pltpu.make_async_copy(bias, biaso, bisem).start()

    n_chunks = jnp.where(swapped, 384 // LNB, 768 // LNB)
    row0 = jnp.where(swapped, zh * 384, 0)
    out0 = jnp.where(swapped, 768, 0)

    def stage(i, s):
        r = pl.multiple_of(row0 + i * LNB, LNB)
        return (
            pltpu.make_async_copy(lat.at[pl.ds(r, LNB)], lstage.at[s], stsem.at[0, s]),
            pltpu.make_async_copy(ctl.at[pl.ds(r, LNB)], cstage.at[s], stsem.at[1, s]),
        )

    for cp in stage(0, 0):
        cp.start()

    def piece(m, half, d, part):
        rows = slice(None) if part is None else pl.ds(part * 80, 80)
        if half == 0:
            return W.at[m, y, (x + 4 - d) % 4, c, rows, pl.ds(0, XCS[m])]
        return W.at[m, (y + 4 - d) % 4, x, c, rows, pl.ds(XCS[m], 640 - XCS[m])]

    def chunk(m, half, d, part=None):
        many = slice(None) if part is None else pl.ds(part * 2, 2)
        if half == 0:
            return W.at[m, (y + 4 - d) % 4, many, c, :, pl.ds(0, XCS[m])]
        return W.at[m, many, (x + 4 - d) % 4, c, :, pl.ds(XCS[m], 640 - XCS[m])]

    def along(axis, way):
        d = 1 if way == 0 else 3
        return place(x + d, y, z, c) if axis == 0 else place(x, y + d, z, c)

    def a_copy(m, half, way, part):
        ref = piece(m, half, 0, part)
        return remote(ref, ref, asem.at[m, half, way, part], arsem.at[m, half, way, part], along(half, way))

    def a_relay(m, half, way):
        ref = piece(m, half, 1 if way == 0 else 3, way)
        return remote(ref, ref, asem.at[m, half, way, 2], arsem.at[m, half, way, 2], along(half, way))

    def b_copy(m, half, way, part):
        ref = chunk(m, half, 0, part)
        return remote(ref, ref, bsem.at[m, half, way, part], brsem.at[m, half, way, part], along(1 - half, way))

    def b_relay(m, half, way):
        ref = chunk(m, half, 1 if way == 0 else 3, way)
        return remote(ref, ref, bsem.at[m, half, way, 2], brsem.at[m, half, way, 2], along(1 - half, way))

    def f_copy(m, half, d):
        ref = chunk(m, half, d)
        return remote(ref, ref, fsem.at[m, half, d], frsem.at[m, half, d], partner)

    def step_a1(m):
        @pl.when(swapped)
        def _():
            remote(ws[m], W.at[m, y, x, c], plsem.at[m], plrsem.at[m], swap_dev).wait()

        @pl.when(jnp.logical_not(swapped))
        def _():
            pltpu.make_async_copy(ws[m], slot(m), plsem.at[m]).wait()

        for part in (0, 1):
            for way in (0, 1):
                for half in (0, 1):
                    a_copy(m, half, way, part ^ way).start()

    def step_a2(m):
        for way in (0, 1):
            for half in (0, 1):
                a_copy(m, half, way, way).wait_recv()
                a_relay(m, half, way).start()

    def step_b1(m):
        for half in (0, 1):
            for way in (0, 1):
                a_copy(m, half, way, 1 - way).wait_recv()
                a_relay(m, half, way).wait_recv()
        for part in (0, 1):
            for way in (0, 1):
                for half in (0, 1):
                    b_copy(m, half, way, part ^ way).start()
        for half in (0, 1):
            f_copy(m, half, 0).start()

    def step_b2(m):
        for way in (0, 1):
            for half in (0, 1):
                b_copy(m, half, way, way).wait_recv()
                b_relay(m, half, way).start()

    def step_f(m):
        for half in (0, 1):
            for way in (0, 1):
                b_copy(m, half, way, 1 - way).wait_recv()
                f_copy(m, half, 1 if way == 0 else 3).start()

    def step_f2(m):
        for half in (0, 1):
            for way in (0, 1):
                b_relay(m, half, way).wait_recv()
            f_copy(m, half, 2).start()

    spot = WO.at[h, x, zl]

    def w_place():
        @pl.when(y != h)
        def _():
            for t in (0, 1):
                remote(wo, spot, rsem.at[t], rrsem.at[zl], swapdev(t)).start()

        @pl.when(y == h)
        def _():
            pltpu.make_async_copy(wo, spot, lsem.at[0]).start()
            remote(wo, spot, rsem.at[0], rrsem.at[zl], swapdev(1 - zl)).start()

    def w_placed():
        @pl.when(y != h)
        def _():
            for t in (0, 1):
                remote(wo, WO.at[y, x, t], rsem.at[t], rrsem.at[t], partner).wait_recv()

        @pl.when(y == h)
        def _():
            pltpu.make_async_copy(wo, spot, lsem.at[0]).wait()
            remote(wo, spot, rsem.at[0], rrsem.at[1 - zl], partner).wait_recv()

    def w_piece(half, d, part):
        rows = pl.ds(part * 80, 80)
        if half == 0:
            return WO.at[y, (x + 4 - d) % 4, 0, rows]
        return WO.at[(y + 4 - d) % 4, x, 1, rows]

    def w_chunk(half, d, part):
        many = pl.ds(part * 2, 2)
        if half == 0:
            return WO.at[(y + 4 - d) % 4, many, 0]
        return WO.at[many, (x + 4 - d) % 4, 1]

    def wa_copy(half, way, part):
        ref = w_piece(half, 0, part)
        return remote(ref, ref, wasem.at[half, way, part], warsem.at[half, way, part], along(half, way))

    def wa_relay(half, way):
        ref = w_piece(half, 1 if way == 0 else 3, way)
        return remote(ref, ref, wasem.at[half, way, 2], warsem.at[half, way, 2], along(half, way))

    def wb_copy(half, way, part):
        ref = w_chunk(half, 0, part)
        return remote(ref, ref, wbsem.at[half, way, part], wbrsem.at[half, way, part], along(1 - half, way))

    def wb_relay(half, way):
        ref = w_chunk(half, 3, way)
        return remote(ref, ref, wbsem.at[half, way, 2], wbrsem.at[half, way, 2], along(1 - half, 1))

    every = [(half, way) for way in (0, 1) for half in (0, 1)]

    def w_a1():
        w_placed()
        for part in (0, 1):
            for half, way in every:
                wa_copy(half, way, part ^ way).start()

    def w_a2():
        for half, way in every:
            wa_copy(half, way, way).wait_recv()
            wa_relay(half, way).start()

    def w_b1():
        for half, way in every:
            wa_copy(half, way, 1 - way).wait_recv()
            wa_relay(half, way).wait_recv()
        for part in (0, 1):
            for half, way in every:
                wb_copy(half, way, part ^ way).start()

    def w_b2():
        for part in (1, 0):
            for half in (0, 1):
                wb_copy(half, 1, part).wait_recv()
                wb_relay(half, part).start()

    def w_done():
        for half, way in every:
            wb_copy(half, 0, way).wait_recv()
        for half, way in every:
            wb_relay(half, way).wait_recv()

    step_a1(0)

    def x_copy(i, by):
        src = N.at[pl.ds(pl.multiple_of(768 + i * LNB, LNB), LNB)]
        dst = N.at[pl.ds(pl.multiple_of(zh * 384 + i * LNB, LNB), LNB)]
        k = 0 if by == 1 else 1
        return remote(src, dst, xsem.at[k, i], xrsem.at[zh, i], place(x, y, z + by, 1 - c))

    def ln_rows(i, s):
        span = jnp.where(swapped, zh, (i * LNB) // 384)

        def body(j, carry):
            r = pl.multiple_of(j * 16, 16)
            hid = lstage[s, pl.ds(r, 16), :].astype(F32) + cstage[s, pl.ds(r, 16), :].astype(F32)
            cen = hid - jnp.mean(hid, axis=-1, keepdims=True)
            var = jnp.mean(cen * cen, axis=-1, keepdims=True)
            nrm = cen * lax.rsqrt(var + 1e-6) * (1.0 + mods[span, 1:2, :]) + mods[span, 0:1, :]
            N[pl.ds(pl.multiple_of(out0 + i * LNB + r, 16), 16), :] = nrm.astype(BF)
            return carry

        lax.fori_loop(0, LNB // 16, body, 0)

    def ln_step(i, carry):
        s = i % 2

        @pl.when(i + 1 < n_chunks)
        def _():
            for cp in stage(i + 1, 1 - s):
                cp.start()

        for cp in stage(i, s):
            cp.wait()
        ln_rows(i, s)

        @pl.when(swapped & (i > 0))
        def _():
            x_copy(i - 1, 1).start()
            x_copy(i - 1, 3).start()

        return carry

    part_chunks = n_chunks // 6
    weave = {0: (step_a1, 1), 1: (step_a2, 0), 2: (step_a1, 2), 3: (step_a2, 1), 4: (step_b1, 0), 5: (step_a2, 2)}
    for seg in range(6):
        lax.fori_loop(seg * part_chunks, (seg + 1) * part_chunks, ln_step, 0)
        fn, m = weave[seg]
        fn(m)

    @pl.when(swapped)
    def _():
        x_copy(384 // LNB - 1, 1).start()
        x_copy(384 // LNB - 1, 3).start()

    def rows_of(r):
        return [pl.ds(pl.multiple_of(s * 384 + r * (TILE // 2), TILE // 2), TILE // 2) for s in (0, 1)]

    def lhs(r, k0, kn):
        return jnp.concatenate([N[rs, pl.ds(k0, kn)] for rs in rows_of(r)], axis=0)

    def put(m, r, cols, val, first):
        for s, rs in enumerate(rows_of(r)):
            part = val[s * (TILE // 2):(s + 1) * (TILE // 2)]
            if first:
                acc[m, rs, cols] = part
            else:
                acc[m, rs, cols] += part

    def x_dot(m, d, r, first):
        yy = (y + 4 - d) % 4
        w = W[m, yy, :, :, :, 0:XCS[m]].reshape(1280, XCS[m])
        v = jnp.dot(lhs(r, pl.multiple_of(yy * 1280, 1280), 1280), w, preferred_element_type=F32)
        put(m, r, slice(0, XCS[m]), v, first)

    def y_dot(m, xp, r, first):
        v = None
        for yy in range(4):
            w = W[m, yy, pl.ds(2 * xp, 2), :, :, XCS[m]:640].reshape(640, 640 - XCS[m])
            t = jnp.dot(lhs(r, pl.multiple_of(yy * 1280 + xp * 640, 640), 640), w, preferred_element_type=F32)
            v = t if v is None else v + t
        put(m, r, slice(XCS[m], 640), v, first)

    def shared(m, half, d):
        f_copy(m, half, d).wait_recv()

    def rows_ready(r):
        @pl.when(swapped)
        def _():
            for span in (0, 1):
                lo = r * (TILE // 2) // LNB
                hi = -(-(r + 1) * (TILE // 2) // LNB)
                prev = -(-r * (TILE // 2) // LNB)
                for i in range(max(lo, prev), hi):
                    src = N.at[pl.ds(768 + i * LNB, LNB)]
                    dst = N.at[pl.ds(span * 384 + i * LNB, LNB)]
                    remote(src, dst, xsem.at[0, i], xrsem.at[span, i], partner).wait_recv()

    def row_sq(m, dst):
        for t in range(6):
            v = acc[m, pl.ds(t * 128, 128), :].astype(BF).astype(F32)
            s = jnp.sum(v * v, axis=-1, keepdims=True)
            wide = jnp.broadcast_to(s, (128, 128))
            sq[dst, :, pl.ds(t * 128, 128)] = jnp.transpose(wide)[0:8, :]

    def s_copy(k, d):
        return remote(
            sq.at[k], sqr.at[k, d - 1], ssem.at[k, d - 1], srsem.at[k, d - 1], place(x, y, z + d, c)
        )

    def normalize(k, m, gain, out):
        for d in (1, 2, 3):
            s_copy(k, d).wait_recv()
        tot = sq[k] + sqr[k, 0] + sqr[k, 1] + sqr[k, 2]
        scale = lax.rsqrt(tot / 2560.0 + 1e-6)
        for t in range(6):
            col = jnp.transpose(jnp.broadcast_to(scale[0:1, t * 128:(t + 1) * 128], (128, 128)))
            rs = pl.ds(t * 128, 128)
            v = acc[m, rs, :].astype(BF).astype(F32)
            out[rs, :] = (v * col[:, 0:1] * biaso[gain:gain + 1, 0:640]).astype(BF)

    def steps(m, kinds, rlo, rhi, fresh):
        for kind, d in kinds:
            if fresh:
                if kind == "x":
                    shared(m, 0, d)
                elif d == 0:
                    for dd in (0, 1, 3):
                        shared(m, 1, dd)
                else:
                    shared(m, 1, 2)

            def body(r, carry, kind=kind, d=d):
                if kind == "x":
                    x_dot(m, d, r, d == 0)
                else:
                    y_dot(m, x // 2 if d == 0 else 1 - x // 2, r, d == 0)
                return carry

            lax.fori_loop(rlo, rhi, body, 0)

    early = (("x", 0), ("x", 1), ("x", 3), ("y", 0))
    late = (("x", 2), ("y", 1))

    def head_cols(i):
        return pl.ds(i * HD, HD)

    def k_copy(t, i, dev):
        return remote(
            (ko, vo)[t].at[:, head_cols(i)], (pko, pvo)[t].at[:, head_cols(i)], ksem.at[t, i], krsem.at[t, i], dev
        )

    step_b2(0)
    step_b1(1)
    step_f(0)
    step_f2(0)
    step_b2(1)
    step_b1(2)
    rows_ready(0)
    rows_ready(1)
    steps(0, early + late, 0, 2, True)
    step_f(1)
    step_f2(1)
    w_place()
    steps(1, early + late, 0, 2, True)
    step_b2(2)
    step_f(2)
    rows_ready(2)
    steps(0, early + late, 2, 3, False)
    steps(1, early + late, 2, 3, False)
    w_a1()
    rows_ready(3)
    steps(0, early + late, 3, 4, False)

    @pl.when(swapped)
    def _():
        remote(bias, biaso, bisem, birsem, swap_dev).wait()

    @pl.when(jnp.logical_not(swapped))
    def _():
        pltpu.make_async_copy(bias, biaso, bisem).wait()

    row_sq(0, 0)
    for d in (1, 3, 2):
        s_copy(0, d).start()
    steps(1, early + late, 3, 4, False)
    for t in range(6):
        rs = pl.ds(t * 128, 128)
        vo[rs, :] = acc[1, rs, :].astype(BF)
    normalize(0, 0, 17, ko)
    step_f2(2)
    w_a2()

    for i in range(5):
        @pl.when(c == 0)
        def _():
            for t in (0, 1):
                k_copy(t, i, partner).start()

        @pl.when(c == 1)
        def _():
            for t in (0, 1):
                k_copy(t, i, nxt).start()

    steps(2, early, 0, 4, True)
    w_b1()
    steps(2, late, 0, 4, True)
    row_sq(2, 1)
    for d in (1, 3, 2):
        s_copy(1, d).start()
    normalize(1, 2, 16, qo)

    cols = pl.ds(pl.multiple_of(h * 1280, 1280), 1280)
    resid = (
        pltpu.make_async_copy(lat.at[:, cols], N.at[pl.ds(0, 768), pl.ds(0, 1280)], lsem.at[1]),
        pltpu.make_async_copy(ctl.at[:, cols], N.at[pl.ds(0, 768), pl.ds(1280, 1280)], lsem.at[2]),
    )
    for cp in resid:
        cp.start()

    mine = c == zl
    fold = HD ** -0.5 * 1.4426950408889634

    def attend_head(i, s):
        cs = head_cols(i)

        ones = jnp.ones((384, HD), BF)
        halves = (pl.ds(0, 384), pl.ds(384, 384))
        srcs = (
            ((pko, pvo, 0), (pko, pvo, 1), (ko, vo, 0)),
            ((pko, pvo, 1), (ko, vo, 0), (ko, vo, 1)),
        )
        for b, (kr, _, part) in enumerate(srcs[s]):
            acc[b, halves[s], 0:384] = lax.dot_general(
                qo[halves[s], cs], kr[halves[part], cs], (((1,), (1,)), ((), ())), preferred_element_type=F32
            )
        if True:
            bs = [biaso[8 * s:8 * s + 1, b * 384:b * 384 + 1] for b in range(3)]
            for t in range(6):
                rs = pl.ds(s * 384 + t * 64, 64)
                blocks = [acc[b, rs, 0:384] for b in range(3)]
                wide = None
                for sc, bv in zip(blocks, bs):
                    w = jnp.maximum(jnp.maximum(sc[:, 0:128], sc[:, 128:256]), sc[:, 256:384]) + bv
                    wide = w if wide is None else jnp.maximum(wide, w)
                top = jnp.max(wide, axis=-1, keepdims=True)
                for b in range(3):
                    ex = jnp.exp2((blocks[b] - (top - bs[b])) * fold)
                    EX[rs, b * 384:(b + 1) * 384] = ex.astype(BF)
            o = None
            for b, (_, vr, part) in enumerate(srcs[s]):
                vv = jnp.concatenate([vr[halves[part], cs], ones], axis=1)
                pv = jnp.dot(EX[halves[s], b * 384:(b + 1) * 384], vv, preferred_element_type=F32)
                o = pv if o is None else o + pv
            qo[halves[s], cs] = (o[:, 0:HD] * (1.0 / o[:, HD:HD + 1])).astype(BF)

    def at_view(ref, u):
        i, sp = u
        return ref.at[pl.ds(sp * 384, 384), head_cols(i)]

    def t_copy(d, u):
        i, sp = u
        return remote(
            at_view(qo, u), at_view(AT.at[z], u), tsem.at[d - 1, sp, i], trsem.at[d - 1, sp, i], place(x, y, z + d, c)
        )

    def own_copy(u):
        i, sp = u
        return pltpu.make_async_copy(at_view(qo, u), at_view(AT.at[z], u), osem.at[sp, i])

    def g_own(u):
        i, sp = u
        return remote(at_view(qo, u), at_view(AT.at[z], u), gsem.at[z, sp, i], grsem.at[z, sp, i], partner)

    def g_copy(g, u):
        i, sp = u
        ref = at_view(AT.at[g], u)
        return remote(ref, ref, gsem.at[g, sp, i], grsem.at[g, sp, i], partner)

    def send_unit(u):
        @pl.when(mine)
        def _():
            t_copy(2, u).start()
            own_copy(u).start()
            g_own(u).start()

        @pl.when(jnp.logical_not(mine))
        def _():
            t_copy(1, u).start()
            t_copy(3, u).start()

    def gather_span(sp):
        @pl.when(mine)
        def _():
            for i in range(5):
                for d in (1, 3, 2):
                    t_copy(d, (i, sp)).wait_recv()
                    g_copy((z + 4 - d) % 4, (i, sp)).start()
            for i in range(5):
                own_copy((i, sp)).wait()

        @pl.when(jnp.logical_not(mine))
        def _():
            for i in range(5):
                for g in range(4):
                    g_copy(g, (i, sp)).wait_recv()

    for sp in (1, 0):
        for i in range(5):
            if sp == 1:
                for t in (0, 1):
                    k_copy(t, i, partner).wait_recv()
            attend_head(i, sp)
            send_unit((i, sp))
        if sp == 1:
            w_b2()
    for cp in resid:
        cp.wait()

    def project_rows(r, n):
        rs = pl.ds(r, n)
        tot = None
        for g in range(4):
            t = lax.dot_general(
                AT[g, rs, :], WO[g].reshape(1280, 640), (((1,), (1,)), ((), ())), preferred_element_type=F32
            ).astype(BF).astype(F32)
            tot = t if tot is None else tot + t
        hid = N[rs, 0:1280].astype(F32) + N[rs, 1280:2560].astype(F32)
        return hid + mods[r // 384, 2:3, cols] * tot

    def h_copy(t):
        rs = pl.ds(t * 192, 192)
        return remote(shout.at[rs], shin.at[rs], hsem.at[t], hrsem.at[t], after)

    gather_span(1)
    w_done()
    for t in (0, 1):
        shout[pl.ds(t * 192, 192), :] = project_rows(384 + t * 192, 192).astype(BF)
        if t:
            h_copy(0).start()
    gather_span(0)
    h_copy(1).start()
    for t in (0, 1):
        out[pl.ds(t * 192, 192), :] = project_rows(t * 192, 192)
    for t in (0, 1):
        h_copy(t).wait_recv()

    for t in (0, 1):
        h_copy(t).wait_send()
    for t in (0, 1):
        for i in range(5):
            k_copy(t, i, partner).wait_send()
    for k in (0, 1):
        for d in (1, 2, 3):
            s_copy(k, d).wait_send()
    for m in range(3):
        for half in (0, 1):
            for way in (0, 1):
                for part in (0, 1):
                    a_copy(m, half, way, part).wait_send()
                    b_copy(m, half, way, part).wait_send()
                a_relay(m, half, way).wait_send()
                b_relay(m, half, way).wait_send()
            for d in range(4):
                f_copy(m, half, d).wait_send()

    @pl.when(swapped)
    def _():
        for i in range(384 // LNB):
            x_copy(i, 1).wait_send()
            x_copy(i, 3).wait_send()

    for half, way in every:
        for part in (0, 1):
            wa_copy(half, way, part).wait_send()
            wb_copy(half, way, part).wait_send()
        wa_relay(half, way).wait_send()
        wb_relay(half, way).wait_send()

    @pl.when(y != h)
    def _():
        for t in (0, 1):
            remote(wo, spot, rsem.at[t], rrsem.at[zl], swapdev(t)).wait_send()

    @pl.when(y == h)
    def _():
        remote(wo, spot, rsem.at[0], rrsem.at[zl], swapdev(1 - zl)).wait_send()

    units = [(i, sp) for sp in (1, 0) for i in range(5)]

    @pl.when(mine)
    def _():
        for u in units:
            t_copy(2, u).wait_send()
            g_own(u).wait_send()
            for d in (1, 2, 3):
                g_copy((z + 4 - d) % 4, u).wait_send()

    @pl.when(jnp.logical_not(mine))
    def _():
        for u in units:
            t_copy(1, u).wait_send()
            t_copy(3, u).wait_send()


def block(lat, ctl, mods, wk, wv, wq, bias, wo):
    any_ = pl.BlockSpec(memory_space=pl.ANY)
    vm = pl.BlockSpec(memory_space=pltpu.VMEM)
    D = pltpu.SemaphoreType.DMA
    rows = pltpu.VMEM((768, 640), BF)
    stage2 = D((3, 2, 2, 3))
    return pl.pallas_call(
        block_kernel,
        out_shape=[jax.ShapeDtypeStruct((384, 1280), F32), jax.ShapeDtypeStruct((384, 1280), BF)],
        in_specs=[any_, any_, vm, any_, any_, any_, any_, any_],
        out_specs=[vm, vm],
        scratch_shapes=[
            pltpu.VMEM((3, 4, 4, 2, 160, 640), BF),
            pltpu.VMEM((1152, 5120), BF),
            pltpu.VMEM((2, LNB, 5120), BF),
            pltpu.VMEM((2, LNB, 5120), BF),
            pltpu.VMEM((3, 768, 640), F32),
            pltpu.VMEM((2, 8, 768), F32),
            pltpu.VMEM((2, 3, 8, 768), F32),
            rows, rows, rows, rows, rows,
            pltpu.VMEM((24, 1152), F32),
            pltpu.VMEM((4, 4, 2, 160, 640), BF),
            pltpu.VMEM((4, 768, 640), BF),
            pltpu.VMEM((384, 1280), BF),
            pltpu.VMEM((768, 1152), BF),
            D((2, 2)), D((3,)), D((3,)),
            stage2, stage2, stage2, stage2, D((3, 2, 4)), D((3, 2, 4)),
            D((2, 384 // LNB)), D((2, 384 // LNB)), D((2, 3)), D((2, 3)), D((2, 5)), D((2, 5)), D, D,
            D((2,)), D((2,)), D((2, 2, 3)), D((2, 2, 3)), D((2, 2, 3)), D((2, 2, 3)),
            D((3, 2, 5)), D((3, 2, 5)), D((4, 2, 5)), D((4, 2, 5)), D((3,)), D((2,)), D((2,)), D((2, 5)),
        ],
        compiler_params=pltpu.CompilerParams(
            collective_id=0, has_side_effects=True, vmem_limit_bytes=67043328
        ),
        name="block",
    )(lat, ctl, mods, wk, wv, wq, bias, wo)


def set_up_kernel(levels, mask, table, qg, kg, mods, aux):
    i = pl.program_id(0)
    row = levels[i] % 8
    for k in range(3):
        mods[0, k:k + 1, :] = table[k, pl.ds(row, 1), :]
    first = lax.axis_index("queue") * 2

    @pl.when(i == 0)
    def _():
        aux[...] = jnp.zeros_like(aux)
        aux[16:17, 0:640] = qg[...].reshape(1, 640)
        aux[17:18, 0:640] = kg[...].reshape(1, 640)
        for s in (0, 1):
            far = (mask[s, 0] == 1) & (first + s >= 2)
            near = (mask[s, 1] == 1) & (first + s >= 1)
            aux[8 * s:8 * s + 8, 0:384] = jnp.full((8, 384), jnp.where(far, 0.0, -1e30), F32)
            aux[8 * s:8 * s + 8, 384:768] = jnp.full((8, 384), jnp.where(near, 0.0, -1e30), F32)


def set_up(levels, window_mask, modulation, q_gain, k_gain):
    gain = pl.BlockSpec((640,), lambda i, levels, mask: (0,))
    return pl.pallas_call(
        set_up_kernel,
        grid_spec=pltpu.PrefetchScalarGridSpec(
            num_scalar_prefetch=2,
            grid=(2,),
            in_specs=[
                pl.BlockSpec((3, 8, 5120), lambda i, levels, mask: (0, levels[i] // 8, 0)),
                gain,
                gain,
            ],
            out_specs=[
                pl.BlockSpec((1, 3, 5120), lambda i, levels, mask: (i, 0, 0)),
                pl.BlockSpec((24, 1152), lambda i, levels, mask: (0, 0)),
            ],
        ),
        out_shape=[jax.ShapeDtypeStruct((2, 3, 5120), F32), jax.ShapeDtypeStruct((24, 1152), F32)],
        name="set_up",
    )(levels, window_mask, jnp.transpose(modulation, (1, 0, 2)), q_gain, k_gain)


def shards(latents, control, levels, window_mask, modulation, w_query, w_key, w_value, w_out, q_gain, k_gain):
    lat = latents.reshape(768, 5120)
    ctl = control.reshape(768, 5120)
    mods, aux = set_up(levels, window_mask, modulation, q_gain, k_gain)
    even, odd = block(lat, ctl, mods, w_key, w_value, w_query, aux, w_out.T)
    return jnp.stack([odd.astype(F32), even])


def solution(mesh):
    placed = (
        P("queue", None, None),
        P("queue", None, None),
        P("queue"),
        P("queue", None),
        P(),
        P("queue", "head"),
        P("queue", "head"),
        P("queue", "head"),
        P("head", "queue"),
        P("head"),
        P("head"),
    )
    return jax.shard_map(
        shards, mesh=mesh, in_specs=placed, out_specs=P("queue", None, "head"), check_vma=False
    )
```

```python
import functools

import jax
import jax.numpy as jnp
from jax import lax
from jax.experimental import pallas as pl
from jax.experimental.pallas import tpu as pltpu
from jax.sharding import PartitionSpec as P

HD = 128
MESH = pl.DeviceIdType.MESH
BF = jnp.bfloat16
F32 = jnp.float32
XCS = (384, 256, 384)
TILE = 192
LNB = 64


def place(x, y, z, c):
    x, y, z = x % 4, y % 4, z % 4
    return ((y * 4 + x) * 2 + z % 2, (z // 2) * 2 + c)


def where_am_i():
    q = lax.axis_index("queue")
    h = lax.axis_index("head")
    return (q // 2) % 4, q // 8, (h // 2) * 2 + q % 2, h % 2


def remote(src, dst, ss, rs, dev):
    return pltpu.make_async_remote_copy(
        src_ref=src, dst_ref=dst, send_sem=ss, recv_sem=rs, device_id=dev, device_id_type=MESH
    )


def block_kernel(
    lat, ctl, mods, wk, wv, wq, bias, wo,
    out, shin,
    W, N, lstage, cstage, acc, sq, sqr, qo, ko, vo, pko, pvo, biaso, WO, AT, shout, EX,
    stsem, plsem, plrsem, asem, arsem, bsem, brsem, fsem, frsem,
    xsem, xrsem, ssem, srsem, ksem, krsem, bisem, birsem,
    rsem, rrsem, wasem, warsem, wbsem, wbrsem, tsem, trsem, gsem, grsem, lsem, hsem, hrsem, osem,
):
    x, y, z, c = where_am_i()
    zl = z % 2
    zh = z // 2
    mine = place(x, y, z, c)
    partner = place(x, y, z, 1 - c)
    swapped = c != zl
    p = y * 4 + x
    pn = (p + 1) % 16
    pp = (p + 15) % 16
    nxt = place(pn % 4, pn // 4, z, 1 - c)
    prv = place(pp % 4, pp // 4, z, 1 - c)

    q = lax.axis_index("queue")
    h = lax.axis_index("head")
    after = ((q + 1) % 32, h)
    before = ((q + 31) % 32, h)
    barrier = pltpu.get_barrier_semaphore()

    def swapdev(t):
        return ((h * 4 + x) * 2 + t, y)


    def greet(dev):
        pl.semaphore_signal(barrier, inc=1, device_id=dev, device_id_type=MESH)

    for d in (1, 2, 3):
        greet(place(x + d, y, z, c))
        greet(place(x, y + d, z, c))
        greet(place(x, y, z + d, c))
    greet(partner)

    @pl.when(c == 1)
    def _():
        greet(nxt)

    @pl.when(c == 0)
    def _():
        greet(prv)

    @pl.when(swapped)
    def _():
        greet(place(x, y, z + 1, 1 - c))
        greet(place(x, y, z + 3, 1 - c))

    @pl.when(y != h)
    def _():
        greet(swapdev(0))
        greet(swapdev(1))

    @pl.when(y == h)
    def _():
        greet(swapdev(1 - zl))

    greet(after)
    greet(before)
    pl.semaphore_wait(barrier, jnp.where(swapped, 13, 11) + jnp.where(y != h, 2, 1) + 2)

    swap_dev = place(x, y, 2 * zh + c, 1 - c)
    ws = (wk, wv, wq)

    def slot(m):
        return W.at[m, y, x, zl]

    @pl.when(swapped)
    def _():
        for m in range(3):
            remote(ws[m], slot(m), plsem.at[m], plrsem.at[m], swap_dev).start()
        remote(bias, biaso, bisem, birsem, swap_dev).start()

    @pl.when(jnp.logical_not(swapped))
    def _():
        for m in range(3):
            pltpu.make_async_copy(ws[m], slot(m), plsem.at[m]).start()
        pltpu.make_async_copy(bias, biaso, bisem).start()

    n_chunks = jnp.where(swapped, 384 // LNB, 768 // LNB)
    row0 = jnp.where(swapped, zh * 384, 0)
    out0 = jnp.where(swapped, 768, 0)

    def stage(i, s):
        r = pl.multiple_of(row0 + i * LNB, LNB)
        return (
            pltpu.make_async_copy(lat.at[pl.ds(r, LNB)], lstage.at[s], stsem.at[0, s]),
            pltpu.make_async_copy(ctl.at[pl.ds(r, LNB)], cstage.at[s], stsem.at[1, s]),
        )

    for cp in stage(0, 0):
        cp.start()

    def piece(m, half, d, part):
        rows = slice(None) if part is None else pl.ds(part * 80, 80)
        if half == 0:
            return W.at[m, y, (x + 4 - d) % 4, c, rows, pl.ds(0, XCS[m])]
        return W.at[m, (y + 4 - d) % 4, x, c, rows, pl.ds(XCS[m], 640 - XCS[m])]

    def chunk(m, half, d, part=None):
        many = slice(None) if part is None else pl.ds(part * 2, 2)
        if half == 0:
            return W.at[m, (y + 4 - d) % 4, many, c, :, pl.ds(0, XCS[m])]
        return W.at[m, many, (x + 4 - d) % 4, c, :, pl.ds(XCS[m], 640 - XCS[m])]

    def along(axis, way):
        d = 1 if way == 0 else 3
        return place(x + d, y, z, c) if axis == 0 else place(x, y + d, z, c)

    def a_copy(m, half, way, part):
        ref = piece(m, half, 0, part)
        return remote(ref, ref, asem.at[m, half, way, part], arsem.at[m, half, way, part], along(half, way))

    def a_relay(m, half, way):
        ref = piece(m, half, 1 if way == 0 else 3, way)
        return remote(ref, ref, asem.at[m, half, way, 2], arsem.at[m, half, way, 2], along(half, way))

    def b_copy(m, half, way, part):
        ref = chunk(m, half, 0, part)
        return remote(ref, ref, bsem.at[m, half, way, part], brsem.at[m, half, way, part], along(1 - half, way))

    def b_relay(m, half, way):
        ref = chunk(m, half, 1 if way == 0 else 3, way)
        return remote(ref, ref, bsem.at[m, half, way, 2], brsem.at[m, half, way, 2], along(1 - half, way))

    def f_copy(m, half, d):
        ref = chunk(m, half, d)
        return remote(ref, ref, fsem.at[m, half, d], frsem.at[m, half, d], partner)

    def step_a1(m):
        @pl.when(swapped)
        def _():
            remote(ws[m], W.at[m, y, x, c], plsem.at[m], plrsem.at[m], swap_dev).wait()

        @pl.when(jnp.logical_not(swapped))
        def _():
            pltpu.make_async_copy(ws[m], slot(m), plsem.at[m]).wait()

        for part in (0, 1):
            for way in (0, 1):
                for half in (0, 1):
                    a_copy(m, half, way, part ^ way).start()

    def step_a2(m):
        for way in (0, 1):
            for half in (0, 1):
                a_copy(m, half, way, way).wait_recv()
                a_relay(m, half, way).start()

    def step_b1(m):
        for half in (0, 1):
            for way in (0, 1):
                a_copy(m, half, way, 1 - way).wait_recv()
                a_relay(m, half, way).wait_recv()
        for part in (0, 1):
            for way in (0, 1):
                for half in (0, 1):
                    b_copy(m, half, way, part ^ way).start()
        for half in (0, 1):
            f_copy(m, half, 0).start()

    def step_b2(m):
        for way in (0, 1):
            for half in (0, 1):
                b_copy(m, half, way, way).wait_recv()
                b_relay(m, half, way).start()

    def step_f(m):
        for half in (0, 1):
            for way in (0, 1):
                b_copy(m, half, way, 1 - way).wait_recv()
                f_copy(m, half, 1 if way == 0 else 3).start()

    def step_f2(m):
        for half in (0, 1):
            for way in (0, 1):
                b_relay(m, half, way).wait_recv()
            f_copy(m, half, 2).start()

    spot = WO.at[h, x, zl]

    def w_place():
        @pl.when(y != h)
        def _():
            for t in (0, 1):
                remote(wo, spot, rsem.at[t], rrsem.at[zl], swapdev(t)).start()

        @pl.when(y == h)
        def _():
            pltpu.make_async_copy(wo, spot, lsem.at[0]).start()
            remote(wo, spot, rsem.at[0], rrsem.at[zl], swapdev(1 - zl)).start()

    def w_placed():
        @pl.when(y != h)
        def _():
            for t in (0, 1):
                remote(wo, WO.at[y, x, t], rsem.at[t], rrsem.at[t], partner).wait_recv()

        @pl.when(y == h)
        def _():
            pltpu.make_async_copy(wo, spot, lsem.at[0]).wait()
            remote(wo, spot, rsem.at[0], rrsem.at[1 - zl], partner).wait_recv()

    def w_piece(half, d, part):
        rows = pl.ds(part * 80, 80)
        if half == 0:
            return WO.at[y, (x + 4 - d) % 4, 0, rows]
        return WO.at[(y + 4 - d) % 4, x, 1, rows]

    def w_chunk(half, d, part):
        many = pl.ds(part * 2, 2)
        if half == 0:
            return WO.at[(y + 4 - d) % 4, many, 0]
        return WO.at[many, (x + 4 - d) % 4, 1]

    def wa_copy(half, way, part):
        ref = w_piece(half, 0, part)
        return remote(ref, ref, wasem.at[half, way, part], warsem.at[half, way, part], along(half, way))

    def wa_relay(half, way):
        ref = w_piece(half, 1 if way == 0 else 3, way)
        return remote(ref, ref, wasem.at[half, way, 2], warsem.at[half, way, 2], along(half, way))

    def wb_copy(half, way, part):
        ref = w_chunk(half, 0, part)
        return remote(ref, ref, wbsem.at[half, way, part], wbrsem.at[half, way, part], along(1 - half, way))

    def wb_relay(half, way):
        ref = w_chunk(half, 3, way)
        return remote(ref, ref, wbsem.at[half, way, 2], wbrsem.at[half, way, 2], along(1 - half, 1))

    every = [(half, way) for way in (0, 1) for half in (0, 1)]

    def w_a1():
        w_placed()
        for part in (0, 1):
            for half, way in every:
                wa_copy(half, way, part ^ way).start()

    def w_a2():
        for half, way in every:
            wa_copy(half, way, way).wait_recv()
            wa_relay(half, way).start()

    def w_b1():
        for half, way in every:
            wa_copy(half, way, 1 - way).wait_recv()
            wa_relay(half, way).wait_recv()
        for part in (0, 1):
            for half, way in every:
                wb_copy(half, way, part ^ way).start()

    def w_b2():
        for part in (1, 0):
            for half in (0, 1):
                wb_copy(half, 1, part).wait_recv()
                wb_relay(half, part).start()

    def w_done():
        for half, way in every:
            wb_copy(half, 0, way).wait_recv()
        for half, way in every:
            wb_relay(half, way).wait_recv()

    step_a1(0)

    def x_copy(i, by):
        src = N.at[pl.ds(pl.multiple_of(768 + i * LNB, LNB), LNB)]
        dst = N.at[pl.ds(pl.multiple_of(zh * 384 + i * LNB, LNB), LNB)]
        k = 0 if by == 1 else 1
        return remote(src, dst, xsem.at[k, i], xrsem.at[zh, i], place(x, y, z + by, 1 - c))

    def ln_rows(i, s):
        span = jnp.where(swapped, zh, (i * LNB) // 384)

        def body(j, carry):
            r = pl.multiple_of(j * 16, 16)
            hid = lstage[s, pl.ds(r, 16), :].astype(F32) + cstage[s, pl.ds(r, 16), :].astype(F32)
            cen = hid - jnp.mean(hid, axis=-1, keepdims=True)
            var = jnp.mean(cen * cen, axis=-1, keepdims=True)
            nrm = cen * lax.rsqrt(var + 1e-6) * (1.0 + mods[span, 1:2, :]) + mods[span, 0:1, :]
            N[pl.ds(pl.multiple_of(out0 + i * LNB + r, 16), 16), :] = nrm.astype(BF)
            return carry

        lax.fori_loop(0, LNB // 16, body, 0, unroll=True)

    def ln_step(i, carry):
        s = i % 2

        @pl.when(i + 1 < n_chunks)
        def _():
            for cp in stage(i + 1, 1 - s):
                cp.start()

        for cp in stage(i, s):
            cp.wait()
        ln_rows(i, s)

        @pl.when(swapped & (i > 0))
        def _():
            x_copy(i - 1, 1).start()
            x_copy(i - 1, 3).start()

        return carry

    part_chunks = n_chunks // 6
    weave = {0: (step_a1, 1), 1: (step_a2, 0), 2: (step_a1, 2), 3: (step_a2, 1), 4: (step_b1, 0), 5: (step_a2, 2)}

    def ln_weave(i, carry):
        ln_step(i, carry)
        for seg, (fn, m) in weave.items():
            @pl.when(i == (seg + 1) * part_chunks - 1)
            def _(fn=fn, m=m):
                fn(m)

        return carry

    lax.fori_loop(0, n_chunks, ln_weave, 0)

    @pl.when(swapped)
    def _():
        x_copy(384 // LNB - 1, 1).start()
        x_copy(384 // LNB - 1, 3).start()

    def rows_of(r):
        return [pl.ds(pl.multiple_of(s * 384 + r * (TILE // 2), TILE // 2), TILE // 2) for s in (0, 1)]

    def lhs(r, k0, kn):
        return jnp.concatenate([N[rs, pl.ds(k0, kn)] for rs in rows_of(r)], axis=0)

    def put(m, r, cols, val, first):
        for s, rs in enumerate(rows_of(r)):
            part = val[s * (TILE // 2):(s + 1) * (TILE // 2)]
            if first:
                acc[m, rs, cols] = part
            else:
                acc[m, rs, cols] += part

    def x_dot(m, d, r, first):
        yy = (y + 4 - d) % 4
        w = W[m, yy, :, :, :, 0:XCS[m]].reshape(1280, XCS[m])
        v = jnp.dot(lhs(r, pl.multiple_of(yy * 1280, 1280), 1280), w, preferred_element_type=F32)
        put(m, r, slice(0, XCS[m]), v, first)

    def y_dot(m, xp, r, first):
        v = None
        for yy in range(4):
            w = W[m, yy, pl.ds(2 * xp, 2), :, :, XCS[m]:640].reshape(640, 640 - XCS[m])
            t = jnp.dot(lhs(r, pl.multiple_of(yy * 1280 + xp * 640, 640), 640), w, preferred_element_type=F32)
            v = t if v is None else v + t
        put(m, r, slice(XCS[m], 640), v, first)

    def shared(m, half, d):
        f_copy(m, half, d).wait_recv()

    def rows_ready(r):
        @pl.when(swapped)
        def _():
            for span in (0, 1):
                lo = r * (TILE // 2) // LNB
                hi = -(-(r + 1) * (TILE // 2) // LNB)
                prev = -(-r * (TILE // 2) // LNB)
                for i in range(max(lo, prev), hi):
                    src = N.at[pl.ds(768 + i * LNB, LNB)]
                    dst = N.at[pl.ds(span * 384 + i * LNB, LNB)]
                    remote(src, dst, xsem.at[0, i], xrsem.at[span, i], partner).wait_recv()

    def row_sq(m, dst):
        for t in range(6):
            v = acc[m, pl.ds(t * 128, 128), :].astype(BF).astype(F32)
            s = jnp.sum(v * v, axis=-1, keepdims=True)
            wide = jnp.broadcast_to(s, (128, 128))
            sq[dst, :, pl.ds(t * 128, 128)] = jnp.transpose(wide)[0:8, :]

    def s_copy(k, d):
        return remote(
            sq.at[k], sqr.at[k, d - 1], ssem.at[k, d - 1], srsem.at[k, d - 1], place(x, y, z + d, c)
        )

    def normalize(k, m, gain, out):
        for d in (1, 2, 3):
            s_copy(k, d).wait_recv()
        tot = sq[k] + sqr[k, 0] + sqr[k, 1] + sqr[k, 2]
        scale = lax.rsqrt(tot / 2560.0 + 1e-6)
        for t in range(6):
            col = jnp.transpose(jnp.broadcast_to(scale[0:1, t * 128:(t + 1) * 128], (128, 128)))
            rs = pl.ds(t * 128, 128)
            v = acc[m, rs, :].astype(BF).astype(F32)
            out[rs, :] = (v * col[:, 0:1] * biaso[gain:gain + 1, 0:640]).astype(BF)

    def steps(m, kinds, rlo, rhi, fresh):
        for kind, d in kinds:
            if fresh:
                if kind == "x":
                    shared(m, 0, d)
                elif d == 0:
                    for dd in (0, 1, 3):
                        shared(m, 1, dd)
                else:
                    shared(m, 1, 2)

            def body(r, carry, kind=kind, d=d):
                if kind == "x":
                    x_dot(m, d, r, d == 0)
                else:
                    y_dot(m, x // 2 if d == 0 else 1 - x // 2, r, d == 0)
                return carry

            lax.fori_loop(rlo, rhi, body, 0)

    early = (("x", 0), ("x", 1), ("x", 3), ("y", 0))
    late = (("x", 2), ("y", 1))

    def head_cols(i):
        return pl.ds(pl.multiple_of(i * HD, HD), HD)

    def k_copy(t, i, dev):
        return remote(
            (ko, vo)[t].at[:, head_cols(i)], (pko, pvo)[t].at[:, head_cols(i)], ksem.at[t, i], krsem.at[t, i], dev
        )

    step_b2(0)
    step_b1(1)
    step_f(0)
    step_f2(0)
    step_b2(1)
    step_b1(2)
    rows_ready(0)
    rows_ready(1)
    steps(0, early + late, 0, 2, True)
    step_f(1)
    step_f2(1)
    w_place()
    steps(1, early + late, 0, 2, True)
    step_b2(2)
    step_f(2)
    rows_ready(2)
    steps(0, early + late, 2, 3, False)
    steps(1, early + late, 2, 3, False)
    w_a1()
    rows_ready(3)
    steps(0, early + late, 3, 4, False)

    @pl.when(swapped)
    def _():
        remote(bias, biaso, bisem, birsem, swap_dev).wait()

    @pl.when(jnp.logical_not(swapped))
    def _():
        pltpu.make_async_copy(bias, biaso, bisem).wait()

    row_sq(0, 0)
    for d in (1, 3, 2):
        s_copy(0, d).start()
    steps(1, early + late, 3, 4, False)
    for t in range(6):
        rs = pl.ds(t * 128, 128)
        vo[rs, :] = acc[1, rs, :].astype(BF)
    normalize(0, 0, 17, ko)
    step_f2(2)
    w_a2()

    for i in range(5):
        @pl.when(c == 0)
        def _():
            for t in (0, 1):
                k_copy(t, i, partner).start()

        @pl.when(c == 1)
        def _():
            for t in (0, 1):
                k_copy(t, i, nxt).start()

    steps(2, early, 0, 4, True)
    w_b1()
    steps(2, late, 0, 4, True)
    row_sq(2, 1)
    for d in (1, 3, 2):
        s_copy(1, d).start()
    normalize(1, 2, 16, qo)

    cols = pl.ds(pl.multiple_of(h * 1280, 1280), 1280)
    resid = (
        pltpu.make_async_copy(lat.at[:, cols], N.at[pl.ds(0, 768), pl.ds(0, 1280)], lsem.at[1]),
        pltpu.make_async_copy(ctl.at[:, cols], N.at[pl.ds(0, 768), pl.ds(1280, 1280)], lsem.at[2]),
    )
    for cp in resid:
        cp.start()

    mine = c == zl
    fold = HD ** -0.5 * 1.4426950408889634

    def attend_head(i, s):
        cs = head_cols(i)

        ones = jnp.ones((384, HD), BF)
        halves = (pl.ds(0, 384), pl.ds(384, 384))
        srcs = (
            ((pko, pvo, 0), (pko, pvo, 1), (ko, vo, 0)),
            ((pko, pvo, 1), (ko, vo, 0), (ko, vo, 1)),
        )
        for b, (kr, _, part) in enumerate(srcs[s]):
            acc[b, halves[s], 0:384] = lax.dot_general(
                qo[halves[s], cs], kr[halves[part], cs], (((1,), (1,)), ((), ())), preferred_element_type=F32
            )
        if True:
            bs = [biaso[8 * s:8 * s + 1, b * 384:b * 384 + 1] for b in range(3)]
            for t in range(6):
                rs = pl.ds(s * 384 + t * 64, 64)
                blocks = [acc[b, rs, 0:384] for b in range(3)]
                wide = None
                for sc, bv in zip(blocks, bs):
                    w = jnp.maximum(jnp.maximum(sc[:, 0:128], sc[:, 128:256]), sc[:, 256:384]) + bv
                    wide = w if wide is None else jnp.maximum(wide, w)
                top = jnp.max(wide, axis=-1, keepdims=True)
                for b in range(3):
                    ex = jnp.exp2((blocks[b] - (top - bs[b])) * fold)
                    EX[rs, b * 384:(b + 1) * 384] = ex.astype(BF)
            o = None
            for b, (_, vr, part) in enumerate(srcs[s]):
                vv = jnp.concatenate([vr[halves[part], cs], ones], axis=1)
                pv = jnp.dot(EX[halves[s], b * 384:(b + 1) * 384], vv, preferred_element_type=F32)
                o = pv if o is None else o + pv
            qo[halves[s], cs] = (o[:, 0:HD] * (1.0 / o[:, HD:HD + 1])).astype(BF)

    def at_view(ref, u):
        i, sp = u
        return ref.at[pl.ds(sp * 384, 384), head_cols(i)]

    def t_copy(d, u):
        i, sp = u
        return remote(
            at_view(qo, u), at_view(AT.at[z], u), tsem.at[d - 1, sp, i], trsem.at[d - 1, sp, i], place(x, y, z + d, c)
        )

    def own_copy(u):
        i, sp = u
        return pltpu.make_async_copy(at_view(qo, u), at_view(AT.at[z], u), osem.at[sp, i])

    def g_own(u):
        i, sp = u
        return remote(at_view(qo, u), at_view(AT.at[z], u), gsem.at[z, sp, i], grsem.at[z, sp, i], partner)

    def g_copy(g, u):
        i, sp = u
        ref = at_view(AT.at[g], u)
        return remote(ref, ref, gsem.at[g, sp, i], grsem.at[g, sp, i], partner)

    def send_unit(u):
        @pl.when(mine)
        def _():
            t_copy(2, u).start()
            own_copy(u).start()
            g_own(u).start()

        @pl.when(jnp.logical_not(mine))
        def _():
            t_copy(1, u).start()
            t_copy(3, u).start()

    def gather_span(sp):
        @pl.when(mine)
        def _():
            for i in range(5):
                for d in (1, 3, 2):
                    t_copy(d, (i, sp)).wait_recv()
                    g_copy((z + 4 - d) % 4, (i, sp)).start()
            for i in range(5):
                own_copy((i, sp)).wait()

        @pl.when(jnp.logical_not(mine))
        def _():
            for i in range(5):
                for g in range(4):
                    g_copy(g, (i, sp)).wait_recv()

    for sp in (1, 0):
        def one_head(i, carry, sp=sp):
            if sp == 1:
                for t in (0, 1):
                    k_copy(t, i, partner).wait_recv()
            attend_head(i, sp)
            send_unit((i, sp))
            return carry

        lax.fori_loop(0, 5, one_head, 0)
        if sp == 1:
            w_b2()
    for cp in resid:
        cp.wait()

    def project_rows(r, n):
        rs = pl.ds(r, n)
        tot = None
        for g in range(4):
            t = lax.dot_general(
                AT[g, rs, :], WO[g].reshape(1280, 640), (((1,), (1,)), ((), ())), preferred_element_type=F32
            ).astype(BF).astype(F32)
            tot = t if tot is None else tot + t
        hid = N[rs, 0:1280].astype(F32) + N[rs, 1280:2560].astype(F32)
        return hid + mods[r // 384, 2:3, cols] * tot

    def h_copy(t):
        rs = pl.ds(t * 192, 192)
        return remote(shout.at[rs], shin.at[rs], hsem.at[t], hrsem.at[t], after)

    gather_span(1)
    w_done()
    for t in (0, 1):
        shout[pl.ds(t * 192, 192), :] = project_rows(384 + t * 192, 192).astype(BF)
        if t:
            h_copy(0).start()
    gather_span(0)
    h_copy(1).start()
    for t in (0, 1):
        out[pl.ds(t * 192, 192), :] = project_rows(t * 192, 192)
    for t in (0, 1):
        h_copy(t).wait_recv()

    for t in (0, 1):
        h_copy(t).wait_send()
    for t in (0, 1):
        for i in range(5):
            k_copy(t, i, partner).wait_send()
    for k in (0, 1):
        for d in (1, 2, 3):
            s_copy(k, d).wait_send()
    for m in range(3):
        for half in (0, 1):
            for way in (0, 1):
                for part in (0, 1):
                    a_copy(m, half, way, part).wait_send()
                    b_copy(m, half, way, part).wait_send()
                a_relay(m, half, way).wait_send()
                b_relay(m, half, way).wait_send()
            for d in range(4):
                f_copy(m, half, d).wait_send()

    @pl.when(swapped)
    def _():
        for i in range(384 // LNB):
            x_copy(i, 1).wait_send()
            x_copy(i, 3).wait_send()

    for half, way in every:
        for part in (0, 1):
            wa_copy(half, way, part).wait_send()
            wb_copy(half, way, part).wait_send()
        wa_relay(half, way).wait_send()
        wb_relay(half, way).wait_send()

    @pl.when(y != h)
    def _():
        for t in (0, 1):
            remote(wo, spot, rsem.at[t], rrsem.at[zl], swapdev(t)).wait_send()

    @pl.when(y == h)
    def _():
        remote(wo, spot, rsem.at[0], rrsem.at[zl], swapdev(1 - zl)).wait_send()

    units = [(i, sp) for sp in (1, 0) for i in range(5)]

    @pl.when(mine)
    def _():
        for u in units:
            t_copy(2, u).wait_send()
            g_own(u).wait_send()
            for d in (1, 2, 3):
                g_copy((z + 4 - d) % 4, u).wait_send()

    @pl.when(jnp.logical_not(mine))
    def _():
        for u in units:
            t_copy(1, u).wait_send()
            t_copy(3, u).wait_send()


def block(lat, ctl, mods, wk, wv, wq, bias, wo):
    any_ = pl.BlockSpec(memory_space=pl.ANY)
    vm = pl.BlockSpec(memory_space=pltpu.VMEM)
    D = pltpu.SemaphoreType.DMA
    rows = pltpu.VMEM((768, 640), BF)
    stage2 = D((3, 2, 2, 3))
    return pl.pallas_call(
        block_kernel,
        out_shape=[jax.ShapeDtypeStruct((384, 1280), F32), jax.ShapeDtypeStruct((384, 1280), BF)],
        in_specs=[any_, any_, vm, any_, any_, any_, any_, any_],
        out_specs=[vm, vm],
        scratch_shapes=[
            pltpu.VMEM((3, 4, 4, 2, 160, 640), BF),
            pltpu.VMEM((1152, 5120), BF),
            pltpu.VMEM((2, LNB, 5120), BF),
            pltpu.VMEM((2, LNB, 5120), BF),
            pltpu.VMEM((3, 768, 640), F32),
            pltpu.VMEM((2, 8, 768), F32),
            pltpu.VMEM((2, 3, 8, 768), F32),
            rows, rows, rows, rows, rows,
            pltpu.VMEM((24, 1152), F32),
            pltpu.VMEM((4, 4, 2, 160, 640), BF),
            pltpu.VMEM((4, 768, 640), BF),
            pltpu.VMEM((384, 1280), BF),
            pltpu.VMEM((768, 1152), BF),
            D((2, 2)), D((3,)), D((3,)),
            stage2, stage2, stage2, stage2, D((3, 2, 4)), D((3, 2, 4)),
            D((2, 384 // LNB)), D((2, 384 // LNB)), D((2, 3)), D((2, 3)), D((2, 5)), D((2, 5)), D, D,
            D((2,)), D((2,)), D((2, 2, 3)), D((2, 2, 3)), D((2, 2, 3)), D((2, 2, 3)),
            D((3, 2, 5)), D((3, 2, 5)), D((4, 2, 5)), D((4, 2, 5)), D((3,)), D((2,)), D((2,)), D((2, 5)),
        ],
        compiler_params=pltpu.CompilerParams(
            collective_id=0, has_side_effects=True, vmem_limit_bytes=67043328
        ),
        name="block",
    )(lat, ctl, mods, wk, wv, wq, bias, wo)


def set_up_kernel(levels, mask, table, qg, kg, mods, aux):
    i = pl.program_id(0)
    row = levels[i] % 8
    for k in range(3):
        mods[0, k:k + 1, :] = table[k, pl.ds(row, 1), :]
    first = lax.axis_index("queue") * 2

    @pl.when(i == 0)
    def _():
        aux[...] = jnp.zeros_like(aux)
        aux[16:17, 0:640] = qg[...].reshape(1, 640)
        aux[17:18, 0:640] = kg[...].reshape(1, 640)
        for s in (0, 1):
            far = (mask[s, 0] == 1) & (first + s >= 2)
            near = (mask[s, 1] == 1) & (first + s >= 1)
            aux[8 * s:8 * s + 8, 0:384] = jnp.full((8, 384), jnp.where(far, 0.0, -1e30), F32)
            aux[8 * s:8 * s + 8, 384:768] = jnp.full((8, 384), jnp.where(near, 0.0, -1e30), F32)


def set_up(levels, window_mask, modulation, q_gain, k_gain):
    gain = pl.BlockSpec((640,), lambda i, levels, mask: (0,))
    return pl.pallas_call(
        set_up_kernel,
        grid_spec=pltpu.PrefetchScalarGridSpec(
            num_scalar_prefetch=2,
            grid=(2,),
            in_specs=[
                pl.BlockSpec((3, 8, 5120), lambda i, levels, mask: (0, levels[i] // 8, 0)),
                gain,
                gain,
            ],
            out_specs=[
                pl.BlockSpec((1, 3, 5120), lambda i, levels, mask: (i, 0, 0)),
                pl.BlockSpec((24, 1152), lambda i, levels, mask: (0, 0)),
            ],
        ),
        out_shape=[jax.ShapeDtypeStruct((2, 3, 5120), F32), jax.ShapeDtypeStruct((24, 1152), F32)],
        name="set_up",
    )(levels, window_mask, jnp.transpose(modulation, (1, 0, 2)), q_gain, k_gain)


def shards(latents, control, levels, window_mask, modulation, w_query, w_key, w_value, w_out, q_gain, k_gain):
    lat = latents.reshape(768, 5120)
    ctl = control.reshape(768, 5120)
    mods, aux = set_up(levels, window_mask, modulation, q_gain, k_gain)
    even, odd = block(lat, ctl, mods, w_key, w_value, w_query, aux, w_out.T)
    return jnp.stack([odd.astype(F32), even])


def solution(mesh):
    placed = (
        P("queue", None, None),
        P("queue", None, None),
        P("queue"),
        P("queue", None),
        P(),
        P("queue", "head"),
        P("queue", "head"),
        P("queue", "head"),
        P("head", "queue"),
        P("head"),
        P("head"),
    )
    return jax.shard_map(
        shards, mesh=mesh, in_specs=placed, out_specs=P("queue", None, "head"), check_vma=False
    )
```

```python
import functools

import jax
import jax.numpy as jnp
from jax import lax
from jax.experimental import pallas as pl
from jax.experimental.pallas import tpu as pltpu
from jax.sharding import PartitionSpec as P

HD = 128
MESH = pl.DeviceIdType.MESH
BF = jnp.bfloat16
F32 = jnp.float32
XCS = (384, 256, 384)
TILE = 192
LNB = 64


def place(x, y, z, c):
    x, y, z = x % 4, y % 4, z % 4
    return ((y * 4 + x) * 2 + z % 2, (z // 2) * 2 + c)


def where_am_i():
    q = lax.axis_index("queue")
    h = lax.axis_index("head")
    return (q // 2) % 4, q // 8, (h // 2) * 2 + q % 2, h % 2


def remote(src, dst, ss, rs, dev):
    return pltpu.make_async_remote_copy(
        src_ref=src, dst_ref=dst, send_sem=ss, recv_sem=rs, device_id=dev, device_id_type=MESH
    )


def block_kernel(
    lat, ctl, mods, wk, wv, wq, bias, wo,
    out, shin,
    W, N, lstage, cstage, acc, sq, sqr, qo, ko, vo, pko, pvo, biaso, WO, AT, shout, EX,
    stsem, plsem, plrsem, asem, arsem, bsem, brsem, fsem, frsem,
    xsem, xrsem, ssem, srsem, ksem, krsem, bisem, birsem,
    rsem, rrsem, wasem, warsem, wbsem, wbrsem, tsem, trsem, gsem, grsem, lsem, hsem, hrsem, osem,
):
    x, y, z, c = where_am_i()
    zl = z % 2
    zh = z // 2
    mine = place(x, y, z, c)
    partner = place(x, y, z, 1 - c)
    swapped = c != zl
    p = y * 4 + x
    pn = (p + 1) % 16
    pp = (p + 15) % 16
    nxt = place(pn % 4, pn // 4, z, 1 - c)
    prv = place(pp % 4, pp // 4, z, 1 - c)

    q = lax.axis_index("queue")
    h = lax.axis_index("head")
    after = ((q + 1) % 32, h)
    before = ((q + 31) % 32, h)
    barrier = pltpu.get_barrier_semaphore()

    def swapdev(t):
        return ((h * 4 + x) * 2 + t, y)


    def greet(dev):
        pl.semaphore_signal(barrier, inc=1, device_id=dev, device_id_type=MESH)

    for d in (1, 2, 3):
        greet(place(x + d, y, z, c))
        greet(place(x, y + d, z, c))
        greet(place(x, y, z + d, c))
    greet(partner)

    @pl.when(c == 1)
    def _():
        greet(nxt)

    @pl.when(c == 0)
    def _():
        greet(prv)

    @pl.when(swapped)
    def _():
        greet(place(x, y, z + 1, 1 - c))
        greet(place(x, y, z + 3, 1 - c))

    @pl.when(y != h)
    def _():
        greet(swapdev(0))
        greet(swapdev(1))

    @pl.when(y == h)
    def _():
        greet(swapdev(1 - zl))

    greet(after)
    greet(before)
    pl.semaphore_wait(barrier, jnp.where(swapped, 13, 11) + jnp.where(y != h, 2, 1) + 2)

    swap_dev = place(x, y, 2 * zh + c, 1 - c)
    ws = (wk, wv, wq)

    def slot(m):
        return W.at[m, y, x, zl]

    @pl.when(swapped)
    def _():
        for m in range(3):
            remote(ws[m], slot(m), plsem.at[m], plrsem.at[m], swap_dev).start()
        remote(bias, biaso, bisem, birsem, swap_dev).start()

    @pl.when(jnp.logical_not(swapped))
    def _():
        for m in range(3):
            pltpu.make_async_copy(ws[m], slot(m), plsem.at[m]).start()
        pltpu.make_async_copy(bias, biaso, bisem).start()

    n_chunks = jnp.where(swapped, 384 // LNB, 768 // LNB)
    row0 = jnp.where(swapped, zh * 384, 0)
    out0 = jnp.where(swapped, 768, 0)

    def stage(i, s):
        r = pl.multiple_of(row0 + i * LNB, LNB)
        return (
            pltpu.make_async_copy(lat.at[pl.ds(r, LNB)], lstage.at[s], stsem.at[0, s]),
            pltpu.make_async_copy(ctl.at[pl.ds(r, LNB)], cstage.at[s], stsem.at[1, s]),
        )

    for cp in stage(0, 0):
        cp.start()

    def piece(m, half, d, part):
        rows = slice(None) if part is None else pl.ds(part * 80, 80)
        if half == 0:
            return W.at[m, y, (x + 4 - d) % 4, c, rows, pl.ds(0, XCS[m])]
        return W.at[m, (y + 4 - d) % 4, x, c, rows, pl.ds(XCS[m], 640 - XCS[m])]

    def chunk(m, half, d, part=None):
        many = slice(None) if part is None else pl.ds(part * 2, 2)
        if half == 0:
            return W.at[m, (y + 4 - d) % 4, many, c, :, pl.ds(0, XCS[m])]
        return W.at[m, many, (x + 4 - d) % 4, c, :, pl.ds(XCS[m], 640 - XCS[m])]

    def along(axis, way):
        d = 1 if way == 0 else 3
        return place(x + d, y, z, c) if axis == 0 else place(x, y + d, z, c)

    def a_copy(m, half, way, part):
        ref = piece(m, half, 0, part)
        return remote(ref, ref, asem.at[m, half, way, part], arsem.at[m, half, way, part], along(half, way))

    def a_relay(m, half, way):
        ref = piece(m, half, 1 if way == 0 else 3, way)
        return remote(ref, ref, asem.at[m, half, way, 2], arsem.at[m, half, way, 2], along(half, way))

    def b_copy(m, half, way, part):
        ref = chunk(m, half, 0, part)
        return remote(ref, ref, bsem.at[m, half, way, part], brsem.at[m, half, way, part], along(1 - half, way))

    def b_relay(m, half, way):
        ref = chunk(m, half, 1 if way == 0 else 3, way)
        return remote(ref, ref, bsem.at[m, half, way, 2], brsem.at[m, half, way, 2], along(1 - half, way))

    def f_copy(m, half, d):
        ref = chunk(m, half, d)
        return remote(ref, ref, fsem.at[m, half, d], frsem.at[m, half, d], partner)

    def step_a1(m):
        @pl.when(swapped)
        def _():
            remote(ws[m], W.at[m, y, x, c], plsem.at[m], plrsem.at[m], swap_dev).wait()

        @pl.when(jnp.logical_not(swapped))
        def _():
            pltpu.make_async_copy(ws[m], slot(m), plsem.at[m]).wait()

        for part in (0, 1):
            for way in (0, 1):
                for half in (0, 1):
                    a_copy(m, half, way, part ^ way).start()

    def step_a2(m):
        for way in (0, 1):
            for half in (0, 1):
                a_copy(m, half, way, way).wait_recv()
                a_relay(m, half, way).start()

    def step_b1(m):
        for half in (0, 1):
            for way in (0, 1):
                a_copy(m, half, way, 1 - way).wait_recv()
                a_relay(m, half, way).wait_recv()
        for part in (0, 1):
            for way in (0, 1):
                for half in (0, 1):
                    b_copy(m, half, way, part ^ way).start()
        for half in (0, 1):
            f_copy(m, half, 0).start()

    def step_b2(m):
        for way in (0, 1):
            for half in (0, 1):
                b_copy(m, half, way, way).wait_recv()
                b_relay(m, half, way).start()

    def step_f(m):
        for half in (0, 1):
            for way in (0, 1):
                b_copy(m, half, way, 1 - way).wait_recv()
                f_copy(m, half, 1 if way == 0 else 3).start()

    def step_f2(m):
        for half in (0, 1):
            for way in (0, 1):
                b_relay(m, half, way).wait_recv()
            f_copy(m, half, 2).start()

    spot = WO.at[h, x, zl]

    def w_place():
        @pl.when(y != h)
        def _():
            for t in (0, 1):
                remote(wo, spot, rsem.at[t], rrsem.at[zl], swapdev(t)).start()

        @pl.when(y == h)
        def _():
            pltpu.make_async_copy(wo, spot, lsem.at[0]).start()
            remote(wo, spot, rsem.at[0], rrsem.at[zl], swapdev(1 - zl)).start()

    def w_placed():
        @pl.when(y != h)
        def _():
            for t in (0, 1):
                remote(wo, WO.at[y, x, t], rsem.at[t], rrsem.at[t], partner).wait_recv()

        @pl.when(y == h)
        def _():
            pltpu.make_async_copy(wo, spot, lsem.at[0]).wait()
            remote(wo, spot, rsem.at[0], rrsem.at[1 - zl], partner).wait_recv()

    def w_piece(half, d, part):
        rows = pl.ds(part * 80, 80)
        if half == 0:
            return WO.at[y, (x + 4 - d) % 4, 0, rows]
        return WO.at[(y + 4 - d) % 4, x, 1, rows]

    def w_chunk(half, d, part):
        many = pl.ds(part * 2, 2)
        if half == 0:
            return WO.at[(y + 4 - d) % 4, many, 0]
        return WO.at[many, (x + 4 - d) % 4, 1]

    def wa_copy(half, way, part):
        ref = w_piece(half, 0, part)
        return remote(ref, ref, wasem.at[half, way, part], warsem.at[half, way, part], along(half, way))

    def wa_relay(half, way):
        ref = w_piece(half, 1 if way == 0 else 3, way)
        return remote(ref, ref, wasem.at[half, way, 2], warsem.at[half, way, 2], along(half, way))

    def wb_copy(half, way, part):
        ref = w_chunk(half, 0, part)
        return remote(ref, ref, wbsem.at[half, way, part], wbrsem.at[half, way, part], along(1 - half, way))

    def wb_relay(half, way):
        ref = w_chunk(half, 3, way)
        return remote(ref, ref, wbsem.at[half, way, 2], wbrsem.at[half, way, 2], along(1 - half, 1))

    every = [(half, way) for way in (0, 1) for half in (0, 1)]

    def w_a1():
        w_placed()
        for part in (0, 1):
            for half, way in every:
                wa_copy(half, way, part ^ way).start()

    def w_a2():
        for half, way in every:
            wa_copy(half, way, way).wait_recv()
            wa_relay(half, way).start()

    def w_b1():
        for half, way in every:
            wa_copy(half, way, 1 - way).wait_recv()
            wa_relay(half, way).wait_recv()
        for part in (0, 1):
            for half, way in every:
                wb_copy(half, way, part ^ way).start()

    def w_b2():
        for part in (1, 0):
            for half in (0, 1):
                wb_copy(half, 1, part).wait_recv()
                wb_relay(half, part).start()

    def w_done():
        for half, way in every:
            wb_copy(half, 0, way).wait_recv()
        for half, way in every:
            wb_relay(half, way).wait_recv()

    step_a1(0)

    def x_copy(i, by):
        src = N.at[pl.ds(pl.multiple_of(768 + i * LNB, LNB), LNB)]
        dst = N.at[pl.ds(pl.multiple_of(zh * 384 + i * LNB, LNB), LNB)]
        k = 0 if by == 1 else 1
        return remote(src, dst, xsem.at[k, i], xrsem.at[zh, i], place(x, y, z + by, 1 - c))

    def ln_rows(i, s):
        span = jnp.where(swapped, zh, (i * LNB) // 384)

        def body(j, carry):
            r = pl.multiple_of(j * 16, 16)
            hid = lstage[s, pl.ds(r, 16), :].astype(F32) + cstage[s, pl.ds(r, 16), :].astype(F32)
            cen = hid - jnp.mean(hid, axis=-1, keepdims=True)
            var = jnp.mean(cen * cen, axis=-1, keepdims=True)
            nrm = cen * lax.rsqrt(var + 1e-6) * (1.0 + mods[span, 1:2, :]) + mods[span, 0:1, :]
            N[pl.ds(pl.multiple_of(out0 + i * LNB + r, 16), 16), :] = nrm.astype(BF)
            return carry

        lax.fori_loop(0, LNB // 16, body, 0, unroll=True)

    def ln_step(i, carry):
        s = i % 2

        @pl.when(i + 1 < n_chunks)
        def _():
            for cp in stage(i + 1, 1 - s):
                cp.start()

        for cp in stage(i, s):
            cp.wait()
        ln_rows(i, s)

        @pl.when(swapped & (i > 0))
        def _():
            x_copy(i - 1, 1).start()
            x_copy(i - 1, 3).start()

        return carry

    part_chunks = n_chunks // 6
    weave = {0: (step_a1, 1), 1: (step_a2, 0), 2: (step_a1, 2), 3: (step_a2, 1), 4: (step_b1, 0), 5: (step_a2, 2)}

    def ln_weave(i, carry):
        ln_step(i, carry)
        for seg, (fn, m) in weave.items():
            @pl.when(i == (seg + 1) * part_chunks - 1)
            def _(fn=fn, m=m):
                fn(m)

        return carry

    lax.fori_loop(0, n_chunks, ln_weave, 0)

    @pl.when(swapped)
    def _():
        x_copy(384 // LNB - 1, 1).start()
        x_copy(384 // LNB - 1, 3).start()

    def rows_of(r):
        return [pl.ds(pl.multiple_of(s * 384 + r * (TILE // 2), TILE // 2), TILE // 2) for s in (0, 1)]

    def lhs(r, k0, kn):
        return jnp.concatenate([N[rs, pl.ds(k0, kn)] for rs in rows_of(r)], axis=0)

    def put(m, r, cols, val, first):
        for s, rs in enumerate(rows_of(r)):
            part = val[s * (TILE // 2):(s + 1) * (TILE // 2)]
            if first:
                acc[m, rs, cols] = part
            else:
                acc[m, rs, cols] += part

    def x_dot(m, d, r, first):
        yy = (y + 4 - d) % 4
        w = W[m, yy, :, :, :, 0:XCS[m]].reshape(1280, XCS[m])
        v = jnp.dot(lhs(r, pl.multiple_of(yy * 1280, 1280), 1280), w, preferred_element_type=F32)
        put(m, r, slice(0, XCS[m]), v, first)

    def y_dot(m, xp, r, first):
        v = None
        for yy in range(4):
            w = W[m, yy, pl.ds(2 * xp, 2), :, :, XCS[m]:640].reshape(640, 640 - XCS[m])
            t = jnp.dot(lhs(r, pl.multiple_of(yy * 1280 + xp * 640, 640), 640), w, preferred_element_type=F32)
            v = t if v is None else v + t
        put(m, r, slice(XCS[m], 640), v, first)

    def shared(m, half, d):
        f_copy(m, half, d).wait_recv()

    def rows_ready(r):
        @pl.when(swapped)
        def _():
            for span in (0, 1):
                lo = r * (TILE // 2) // LNB
                hi = -(-(r + 1) * (TILE // 2) // LNB)
                prev = -(-r * (TILE // 2) // LNB)
                for i in range(max(lo, prev), hi):
                    src = N.at[pl.ds(768 + i * LNB, LNB)]
                    dst = N.at[pl.ds(span * 384 + i * LNB, LNB)]
                    remote(src, dst, xsem.at[0, i], xrsem.at[span, i], partner).wait_recv()

    def row_sq(m, dst):
        for t in range(6):
            v = acc[m, pl.ds(t * 128, 128), :].astype(BF).astype(F32)
            s = jnp.sum(v * v, axis=-1, keepdims=True)
            wide = jnp.broadcast_to(s, (128, 128))
            sq[dst, :, pl.ds(t * 128, 128)] = jnp.transpose(wide)[0:8, :]

    def s_copy(k, d):
        return remote(
            sq.at[k], sqr.at[k, d - 1], ssem.at[k, d - 1], srsem.at[k, d - 1], place(x, y, z + d, c)
        )

    def normalize(k, m, gain, out):
        for d in (1, 2, 3):
            s_copy(k, d).wait_recv()
        tot = sq[k] + sqr[k, 0] + sqr[k, 1] + sqr[k, 2]
        scale = lax.rsqrt(tot / 2560.0 + 1e-6)
        for t in range(6):
            col = jnp.transpose(jnp.broadcast_to(scale[0:1, t * 128:(t + 1) * 128], (128, 128)))
            rs = pl.ds(t * 128, 128)
            v = acc[m, rs, :].astype(BF).astype(F32)
            out[rs, :] = (v * col[:, 0:1] * biaso[gain:gain + 1, 0:640]).astype(BF)

    def steps(m, kinds, rlo, rhi, fresh):
        for kind, d in kinds:
            if fresh:
                if kind == "x":
                    shared(m, 0, d)
                elif d == 0:
                    for dd in (0, 1, 3):
                        shared(m, 1, dd)
                else:
                    shared(m, 1, 2)

            def body(r, carry, kind=kind, d=d):
                if kind == "x":
                    x_dot(m, d, r, d == 0)
                else:
                    y_dot(m, x // 2 if d == 0 else 1 - x // 2, r, d == 0)
                return carry

            lax.fori_loop(rlo, rhi, body, 0)

    early = (("x", 0), ("x", 1), ("x", 3), ("y", 0))
    late = (("x", 2), ("y", 1))

    def head_cols(i):
        return pl.ds(pl.multiple_of(i * HD, HD), HD)

    def k_copy(t, i, dev):
        return remote(
            (ko, vo)[t].at[:, head_cols(i)], (pko, pvo)[t].at[:, head_cols(i)], ksem.at[t, i], krsem.at[t, i], dev
        )

    step_b2(0)
    step_b1(1)
    step_f(0)
    step_f2(0)
    step_b2(1)
    step_b1(2)
    rows_ready(0)
    rows_ready(1)
    steps(0, early + late, 0, 2, True)
    step_f(1)
    step_f2(1)
    w_place()
    steps(1, early + late, 0, 2, True)
    step_b2(2)
    step_f(2)
    rows_ready(2)
    steps(0, early + late, 2, 3, False)
    steps(1, early + late, 2, 3, False)
    w_a1()
    rows_ready(3)
    steps(0, early + late, 3, 4, False)

    @pl.when(swapped)
    def _():
        remote(bias, biaso, bisem, birsem, swap_dev).wait()

    @pl.when(jnp.logical_not(swapped))
    def _():
        pltpu.make_async_copy(bias, biaso, bisem).wait()

    row_sq(0, 0)
    for d in (1, 3, 2):
        s_copy(0, d).start()
    steps(1, early + late, 3, 4, False)
    for t in range(6):
        rs = pl.ds(t * 128, 128)
        vo[rs, :] = acc[1, rs, :].astype(BF)
    normalize(0, 0, 17, ko)
    step_f2(2)
    w_a2()

    for i in range(5):
        @pl.when(c == 0)
        def _():
            for t in (0, 1):
                k_copy(t, i, partner).start()

        @pl.when(c == 1)
        def _():
            for t in (0, 1):
                k_copy(t, i, nxt).start()

    steps(2, early, 0, 4, True)
    w_b1()
    steps(2, late, 0, 4, True)
    row_sq(2, 1)
    for d in (1, 3, 2):
        s_copy(1, d).start()
    normalize(1, 2, 16, qo)

    cols = pl.ds(pl.multiple_of(h * 1280, 1280), 1280)
    resid = (
        pltpu.make_async_copy(lat.at[:, cols], N.at[pl.ds(0, 768), pl.ds(0, 1280)], lsem.at[1]),
        pltpu.make_async_copy(ctl.at[:, cols], N.at[pl.ds(0, 768), pl.ds(1280, 1280)], lsem.at[2]),
    )
    for cp in resid:
        cp.start()

    mine = c == zl
    fold = HD ** -0.5 * 1.4426950408889634

    def attend_head(i, s):
        cs = head_cols(i)

        ones = jnp.ones((384, HD), BF)
        halves = (pl.ds(0, 384), pl.ds(384, 384))
        srcs = (
            ((pko, pvo, 0), (pko, pvo, 1), (ko, vo, 0)),
            ((pko, pvo, 1), (ko, vo, 0), (ko, vo, 1)),
        )
        for b, (kr, _, part) in enumerate(srcs[s]):
            acc[b, halves[s], 0:384] = lax.dot_general(
                qo[halves[s], cs], kr[halves[part], cs], (((1,), (1,)), ((), ())), preferred_element_type=F32
            )
        if True:
            bs = [biaso[8 * s:8 * s + 1, b * 384:b * 384 + 1] for b in range(3)]
            for t in range(6):
                rs = pl.ds(s * 384 + t * 64, 64)
                blocks = [acc[b, rs, 0:384] for b in range(3)]
                wide = None
                for sc, bv in zip(blocks, bs):
                    w = jnp.maximum(jnp.maximum(sc[:, 0:128], sc[:, 128:256]), sc[:, 256:384]) + bv
                    wide = w if wide is None else jnp.maximum(wide, w)
                top = jnp.max(wide, axis=-1, keepdims=True)
                for b in range(3):
                    ex = jnp.exp2((blocks[b] - (top - bs[b])) * fold)
                    EX[rs, b * 384:(b + 1) * 384] = ex.astype(BF)
            o = None
            for b, (_, vr, part) in enumerate(srcs[s]):
                vv = jnp.concatenate([vr[halves[part], cs], ones], axis=1)
                pv = jnp.dot(EX[halves[s], b * 384:(b + 1) * 384], vv, preferred_element_type=F32)
                o = pv if o is None else o + pv
            qo[halves[s], cs] = (o[:, 0:HD] * (1.0 / o[:, HD:HD + 1])).astype(BF)

    def at_view(ref, u):
        i, sp = u
        return ref.at[pl.ds(sp * 384, 384), head_cols(i)]

    def t_copy(d, u):
        i, sp = u
        return remote(
            at_view(qo, u), at_view(AT.at[z], u), tsem.at[d - 1, sp, i], trsem.at[d - 1, sp, i], place(x, y, z + d, c)
        )

    def own_copy(u):
        i, sp = u
        return pltpu.make_async_copy(at_view(qo, u), at_view(AT.at[z], u), osem.at[sp, i])

    def g_own(u):
        i, sp = u
        return remote(at_view(qo, u), at_view(AT.at[z], u), gsem.at[z, sp, i], grsem.at[z, sp, i], partner)

    def g_copy(g, u):
        i, sp = u
        ref = at_view(AT.at[g], u)
        return remote(ref, ref, gsem.at[g, sp, i], grsem.at[g, sp, i], partner)

    def send_unit(u):
        @pl.when(mine)
        def _():
            t_copy(2, u).start()
            own_copy(u).start()
            g_own(u).start()

        @pl.when(jnp.logical_not(mine))
        def _():
            t_copy(1, u).start()
            t_copy(3, u).start()

    def gather_span(sp, heads=range(5)):
        @pl.when(mine)
        def _():
            for i in heads:
                for d in (1, 3, 2):
                    t_copy(d, (i, sp)).wait_recv()
                    g_copy((z + 4 - d) % 4, (i, sp)).start()
            for i in heads:
                own_copy((i, sp)).wait()

        @pl.when(jnp.logical_not(mine))
        def _():
            for i in heads:
                for g in range(4):
                    g_copy(g, (i, sp)).wait_recv()

    for sp in (1, 0):
        def one_head(i, carry, sp=sp):
            if sp == 1:
                for t in (0, 1):
                    k_copy(t, i, partner).wait_recv()
            attend_head(i, sp)
            send_unit((i, sp))
            return carry

        lax.fori_loop(0, 5, one_head, 0)
        if sp == 1:
            w_b2()
    for cp in resid:
        cp.wait()

    def project_rows(r, n):
        rs = pl.ds(r, n)
        tot = None
        for g in range(4):
            t = lax.dot_general(
                AT[g, rs, :], WO[g].reshape(1280, 640), (((1,), (1,)), ((), ())), preferred_element_type=F32
            ).astype(BF).astype(F32)
            tot = t if tot is None else tot + t
        hid = N[rs, 0:1280].astype(F32) + N[rs, 1280:2560].astype(F32)
        return hid + mods[r // 384, 2:3, cols] * tot

    def h_copy(t):
        rs = pl.ds(t * 192, 192)
        return remote(shout.at[rs], shin.at[rs], hsem.at[t], hrsem.at[t], after)

    gather_span(1)
    w_done()
    for t in (0, 1):
        shout[pl.ds(t * 192, 192), :] = project_rows(384 + t * 192, 192).astype(BF)
        if t:
            h_copy(0).start()
    gather_span(0, range(1))
    h_copy(1).start()
    gather_span(0, range(1, 5))
    for t in (0, 1):
        out[pl.ds(t * 192, 192), :] = project_rows(t * 192, 192)
    for t in (0, 1):
        h_copy(t).wait_recv()

    for t in (0, 1):
        h_copy(t).wait_send()
    for t in (0, 1):
        for i in range(5):
            k_copy(t, i, partner).wait_send()
    for k in (0, 1):
        for d in (1, 2, 3):
            s_copy(k, d).wait_send()
    for m in range(3):
        for half in (0, 1):
            for way in (0, 1):
                for part in (0, 1):
                    a_copy(m, half, way, part).wait_send()
                    b_copy(m, half, way, part).wait_send()
                a_relay(m, half, way).wait_send()
                b_relay(m, half, way).wait_send()
            for d in range(4):
                f_copy(m, half, d).wait_send()

    @pl.when(swapped)
    def _():
        for i in range(384 // LNB):
            x_copy(i, 1).wait_send()
            x_copy(i, 3).wait_send()

    for half, way in every:
        for part in (0, 1):
            wa_copy(half, way, part).wait_send()
            wb_copy(half, way, part).wait_send()
        wa_relay(half, way).wait_send()
        wb_relay(half, way).wait_send()

    @pl.when(y != h)
    def _():
        for t in (0, 1):
            remote(wo, spot, rsem.at[t], rrsem.at[zl], swapdev(t)).wait_send()

    @pl.when(y == h)
    def _():
        remote(wo, spot, rsem.at[0], rrsem.at[zl], swapdev(1 - zl)).wait_send()

    units = [(i, sp) for sp in (1, 0) for i in range(5)]

    @pl.when(mine)
    def _():
        for u in units:
            t_copy(2, u).wait_send()
            g_own(u).wait_send()
            for d in (1, 2, 3):
                g_copy((z + 4 - d) % 4, u).wait_send()

    @pl.when(jnp.logical_not(mine))
    def _():
        for u in units:
            t_copy(1, u).wait_send()
            t_copy(3, u).wait_send()


def block(lat, ctl, mods, wk, wv, wq, bias, wo):
    any_ = pl.BlockSpec(memory_space=pl.ANY)
    vm = pl.BlockSpec(memory_space=pltpu.VMEM)
    D = pltpu.SemaphoreType.DMA
    rows = pltpu.VMEM((768, 640), BF)
    stage2 = D((3, 2, 2, 3))
    return pl.pallas_call(
        block_kernel,
        out_shape=[jax.ShapeDtypeStruct((384, 1280), F32), jax.ShapeDtypeStruct((384, 1280), BF)],
        in_specs=[any_, any_, vm, any_, any_, any_, any_, any_],
        out_specs=[vm, vm],
        scratch_shapes=[
            pltpu.VMEM((3, 4, 4, 2, 160, 640), BF),
            pltpu.VMEM((1152, 5120), BF),
            pltpu.VMEM((2, LNB, 5120), BF),
            pltpu.VMEM((2, LNB, 5120), BF),
            pltpu.VMEM((3, 768, 640), F32),
            pltpu.VMEM((2, 8, 768), F32),
            pltpu.VMEM((2, 3, 8, 768), F32),
            rows, rows, rows, rows, rows,
            pltpu.VMEM((24, 1152), F32),
            pltpu.VMEM((4, 4, 2, 160, 640), BF),
            pltpu.VMEM((4, 768, 640), BF),
            pltpu.VMEM((384, 1280), BF),
            pltpu.VMEM((768, 1152), BF),
            D((2, 2)), D((3,)), D((3,)),
            stage2, stage2, stage2, stage2, D((3, 2, 4)), D((3, 2, 4)),
            D((2, 384 // LNB)), D((2, 384 // LNB)), D((2, 3)), D((2, 3)), D((2, 5)), D((2, 5)), D, D,
            D((2,)), D((2,)), D((2, 2, 3)), D((2, 2, 3)), D((2, 2, 3)), D((2, 2, 3)),
            D((3, 2, 5)), D((3, 2, 5)), D((4, 2, 5)), D((4, 2, 5)), D((3,)), D((2,)), D((2,)), D((2, 5)),
        ],
        compiler_params=pltpu.CompilerParams(
            collective_id=0, has_side_effects=True, vmem_limit_bytes=67043328
        ),
        name="block",
    )(lat, ctl, mods, wk, wv, wq, bias, wo)


def set_up_kernel(levels, mask, table, qg, kg, mods, aux):
    i = pl.program_id(0)
    row = levels[i] % 8
    for k in range(3):
        mods[0, k:k + 1, :] = table[k, pl.ds(row, 1), :]
    first = lax.axis_index("queue") * 2

    @pl.when(i == 0)
    def _():
        aux[...] = jnp.zeros_like(aux)
        aux[16:17, 0:640] = qg[...].reshape(1, 640)
        aux[17:18, 0:640] = kg[...].reshape(1, 640)
        for s in (0, 1):
            far = (mask[s, 0] == 1) & (first + s >= 2)
            near = (mask[s, 1] == 1) & (first + s >= 1)
            aux[8 * s:8 * s + 8, 0:384] = jnp.full((8, 384), jnp.where(far, 0.0, -1e30), F32)
            aux[8 * s:8 * s + 8, 384:768] = jnp.full((8, 384), jnp.where(near, 0.0, -1e30), F32)


def set_up(levels, window_mask, modulation, q_gain, k_gain):
    gain = pl.BlockSpec((640,), lambda i, levels, mask: (0,))
    return pl.pallas_call(
        set_up_kernel,
        grid_spec=pltpu.PrefetchScalarGridSpec(
            num_scalar_prefetch=2,
            grid=(2,),
            in_specs=[
                pl.BlockSpec((3, 8, 5120), lambda i, levels, mask: (0, levels[i] // 8, 0)),
                gain,
                gain,
            ],
            out_specs=[
                pl.BlockSpec((1, 3, 5120), lambda i, levels, mask: (i, 0, 0)),
                pl.BlockSpec((24, 1152), lambda i, levels, mask: (0, 0)),
            ],
        ),
        out_shape=[jax.ShapeDtypeStruct((2, 3, 5120), F32), jax.ShapeDtypeStruct((24, 1152), F32)],
        name="set_up",
    )(levels, window_mask, jnp.transpose(modulation, (1, 0, 2)), q_gain, k_gain)


def shards(latents, control, levels, window_mask, modulation, w_query, w_key, w_value, w_out, q_gain, k_gain):
    lat = latents.reshape(768, 5120)
    ctl = control.reshape(768, 5120)
    mods, aux = set_up(levels, window_mask, modulation, q_gain, k_gain)
    even, odd = block(lat, ctl, mods, w_key, w_value, w_query, aux, w_out.T)
    return jnp.stack([odd.astype(F32), even])


def solution(mesh):
    placed = (
        P("queue", None, None),
        P("queue", None, None),
        P("queue"),
        P("queue", None),
        P(),
        P("queue", "head"),
        P("queue", "head"),
        P("queue", "head"),
        P("head", "queue"),
        P("head"),
        P("head"),
    )
    return jax.shard_map(
        shards, mesh=mesh, in_specs=placed, out_specs=P("queue", None, "head"), check_vma=False
    )
```
